32 devices in a mesh: pitch: 2 (over core), axial: 4 (over y, x), span: 4 (over z).
Axes of the slice: x: 2, y: 2, z: 4, core: 2. Of those that a mesh axis runs over, the one named last changes fastest.
Arguments:
- state: float32 [5, 16, 128, 512], P(None, 'pitch', 'axial', 'span'), as said below
- coeffs: float32 [2, 4, 5, 128, 512], P(None, None, None, 'axial', 'span'), may hold values from -3 to 3
- lag_shift: int32 [1], replicated, may hold values from 0 to 63
- harmonics: int32 [512], P('span'), may hold values from 1 to 4
Outputs:
- new_state: float32 [5, 16, 128, 512], P(None, 'pitch', 'axial', 'span')
The draws below stay inside these ranges and needn't reach their ends.
Inputs may be any that keep to these rules, and one draw needn't show every extreme that they name: `state`: density lies in 0.8 to 1.25, momenta within -1.5 to 1.5, total energy within 1.6 to 3.4.
All inputs are finite; a program needn't handle non-finite values.
Results may differ from the reference program's by a relative error of at most 0.0001.
Values sent between devices are 32-bit elements; how exact they have to be, the bound alone decides.
A program may use at most 64 MiB of HBM per device.

```python
import math
import jax
import jax.numpy as jnp

FIELDS = 5
HARM_MAX = 4
PERIOD_SAMPLES = 64
NPITCH = 16
NAXIAL = 128
NSPAN = 512
DIFF_NUMBER = 4


def draw_state(key, part):
    keys = jax.random.split(key, 3)
    shape_cells = (NPITCH, NAXIAL, NSPAN)
    density = jax.random.uniform(keys[0], shape_cells, jnp.float32, 0.8, 1.25)
    momentum = 0.5 * jax.random.truncated_normal(keys[1], -3.0, 3.0, (3,) + shape_cells, jnp.float32)
    energy = 2.5 + 0.3 * jax.random.truncated_normal(keys[2], -3.0, 3.0, shape_cells, jnp.float32)
    return jnp.concatenate([density[None], momentum, energy[None]], axis=0)


def plant(values, key, smallest, top_value):
    longest = values.shape.index(max(values.shape))
    spots = []
    for shift in (0, 1):
        where = [jax.random.randint(jax.random.fold_in(key, axis), (), 0, length) for axis, length in enumerate(values.shape)]
        where[longest] = (where[longest] + shift) % values.shape[longest]
        spots.append(tuple(where))
    return values.at[spots[0]].set(smallest).at[spots[1]].set(top_value)


def level_of(own_key, extent, cuts, smallest, high):
    factor_of = 1.0
    for dim, blocks in cuts:
        draws = jax.random.uniform(jax.random.fold_in(jax.random.fold_in(own_key, 6), dim), (blocks,), jnp.float32, smallest / len(cuts), high / len(cuts))
        factor_of = factor_of * jnp.repeat(jnp.exp(draws), extent[dim] // blocks).reshape((-1,) + (1,) * (len(extent) - 1 - dim))
    return factor_of


def gaussian(key, extent, scale, bound, pieces=(), kind=jnp.bfloat16):
    values = jax.random.normal(key, extent, jnp.float32) * scale
    if len(pieces) > 0:
        values = level_of(key, extent, pieces, -0.22, 0.18) * values
    return jnp.clip(values, min=-bound, max=bound).astype(kind)


def setup_inputs(seed: int = 0) -> dict:
    key_of = jax.random.split(jax.random.key(seed), 5)
    return {
        "state": draw_state(jax.random.fold_in(key_of[4], 71), 0),
        "coeffs": gaussian(key_of[1], (2, HARM_MAX, FIELDS, NAXIAL, NSPAN), 0.5, 3.0, ((3, 4), (4, 4)), jnp.float32),
        "lag_shift": jax.random.randint(key_of[2], (1,), 0, PERIOD_SAMPLES).astype(jnp.int32),
        "harmonics": plant(jax.random.randint(key_of[3], (NSPAN,), 1, HARM_MAX + 1), jax.random.fold_in(key_of[3], 1), 1, HARM_MAX).astype(jnp.int32),
    }


HEAT_RATIO_GAS = 1.4
STEP_RATE = 0.25
DAMPING = 0.5
STENCIL = (1.0, -8.0, 28.0, -56.0, 70.0, -56.0, 28.0, -8.0, 1.0)


def pitch_flux(state):
    density = state[0]
    speed = state[2] / density
    kinetic = 0.5 * (state[1] * state[1] + state[2] * state[2] + state[3] * state[3]) / density
    pressure = (HEAT_RATIO_GAS - 1.0) * (state[4] - kinetic)
    return jnp.stack([state[2], state[1] * speed, state[2] * speed + pressure, state[3] * speed, (state[4] + pressure) * speed])


def seam_jump(coeffs, lag_shift, harmonics):
    order = jnp.arange(HARM_MAX)
    phase = (2.0 * math.pi / PERIOD_SAMPLES) * (order + 1).astype(jnp.float32) * lag_shift[0].astype(jnp.float32)
    active = (order[:, None] < harmonics[None, :]).astype(jnp.float32)
    cosine = active * jnp.cos(phase)[:, None]
    sine = active * jnp.sin(phase)[:, None]
    first = jnp.sum(cosine[:, None, None, :] * coeffs[0], axis=0)
    second = jnp.sum(sine[:, None, None, :] * coeffs[1], axis=0)
    return first + second


def damping_from(extended, naxial, nspan):
    along = jnp.zeros_like(extended[:, :, 4:4 + naxial, 4:4 + nspan])
    across = jnp.zeros_like(along)
    for displacement in range(9):
        along = along + STENCIL[displacement] * extended[:, :, displacement:displacement + naxial, 4:4 + nspan]
        across = across + STENCIL[displacement] * extended[:, :, 4:4 + naxial, displacement:displacement + nspan]
    return (along + across) / 256.0


def cyclic_tridiagonal_solve(values, operator_symbol):
    results = []
    for field in range(FIELDS):
        spectrum = jnp.fft.fft(values[field], axis=0) / operator_symbol
        results.append(jnp.real(jnp.fft.ifft(spectrum, axis=0)).astype(jnp.float32))
    return jnp.stack(results)


def reference(state, coeffs, lag_shift, harmonics):
    flux = pitch_flux(state)
    jump = seam_jump(coeffs, lag_shift, harmonics)
    rhs = 0.75 * (jnp.roll(flux, -1, axis=1) - jnp.roll(flux, 1, axis=1))
    rhs = rhs.at[:, 0].add(0.75 * jump)
    rhs = rhs.at[:, -1].add(0.75 * jump)
    wave = (2.0 * math.pi / NPITCH) * jnp.arange(NPITCH).astype(jnp.float32)
    compact_symbol = (1.0 + 0.5 * jnp.cos(wave)).reshape(NPITCH, 1, 1)
    diffusion = float(DIFF_NUMBER)
    relax_symbol = (1.0 + 2.0 * diffusion * (1.0 - jnp.cos(wave))).reshape(NPITCH, 1, 1)
    deriv = cyclic_tridiagonal_solve(rhs, compact_symbol)
    smoothed_increment = cyclic_tridiagonal_solve(state, relax_symbol)
    extended = jnp.pad(state, ((0, 0), (0, 0), (4, 4), (4, 4)))
    damp = damping_from(extended, state.shape[2], state.shape[3])
    return smoothed_increment - STEP_RATE * deriv - DAMPING * damp
```

```python
import functools
import math

import jax
import jax.numpy as jnp
from jax import lax
from jax.experimental import pallas as pl
from jax.experimental.pallas import tpu as pltpu
from jax.sharding import PartitionSpec as P

PERIOD_SAMPLES = 64
HEAT_RATIO_GAS = 1.4
STEP_RATE = 0.25
DAMPING = 0.5
EDGE = (1.0, -8.0, 28.0, -56.0)
MESH = pl.DeviceIdType.MESH


def line_root(main, side):
    root = (-main + math.sqrt(main * main - 4.0 * side * side)) / (2.0 * side)
    return root, 1.0 / (main + 2.0 * side * root)


def pick(position, values):
    chosen = jnp.float32(values[-1])
    for index in range(len(values) - 1):
        chosen = jnp.where(position == index, jnp.float32(values[index]), chosen)
    return chosen


def kernel(
    sizes,
    lag_hbm,
    harm_hbm,
    state_hbm,
    coef_hbm,
    out_ref,
    u,
    co,
    flux,
    sums,
    got_sums,
    ax_own,
    ax_got,
    sp_own,
    got_left,
    got_right,
    waves,
    lag_ref,
    harm_ref,
    pitch_ready,
    span_ready,
    odd_ready,
    even_ready,
    local_sem,
    send_sem,
    recv_sem,
):
    npitch, naxial, nspan = sizes
    fields, cells, rows, _ = u.shape
    tiles = rows // 8
    harm_max = co.shape[1]
    total = cells * npitch
    diffusion = float(total * total // 64)
    r, r_scale = line_root(1.0, 0.25)
    q, q_scale = line_root(1.0 + 2.0 * diffusion, -diffusion)
    pitch, axial, span = (lax.axis_index(name) for name in ("pitch", "axial", "span"))

    state_copies = [
        pltpu.make_async_copy(state_hbm.at[f], u.at[f], local_sem.at[3 + f]) for f in range(fields)
    ]
    coef_copy = pltpu.make_async_copy(coef_hbm, co, local_sem.at[0])
    small_copies = [
        pltpu.make_async_copy(lag_hbm, lag_ref, local_sem.at[1]),
        pltpu.make_async_copy(harm_hbm, harm_ref, local_sem.at[2]),
    ]

    def when(flag, action):
        @pl.when(flag)
        def _():
            action()

    def both(*flags):
        return functools.reduce(jnp.logical_and, flags)

    def no(flag):
        return jnp.logical_not(flag)

    paired = npitch % 2 == 0
    has_up, has_down = axial > 0, axial < naxial - 1
    has_left, has_right = span > 0, span < nspan - 1
    odd = lax.rem(axial, 2) == 1
    even = no(odd)
    hub_block = both(even, axial + 2 < naxial)
    last_even = both(even, axial + 2 >= naxial)
    second = lax.rem(pitch, 2) == 1 if paired else pitch >= 0
    first = no(second)
    hub = both(hub_block, second)
    under_hub = both(odd, has_down)

    barrier = pltpu.get_barrier_semaphore()

    def tell(semaphore, **where):
        pl.semaphore_signal(semaphore, inc=1, device_id=where, device_id_type=MESH)

    def count(*flags):
        return sum(jnp.where(flag, 1, 0) for flag in flags)

    when(both(odd, no(both(has_down, first))), lambda: tell(barrier, axial=axial - 1))
    when(under_hub, lambda: tell(barrier, axial=axial + 1))
    when(both(even, has_down), lambda: tell(barrier, axial=axial + 1))
    when(both(even, has_up, second), lambda: tell(barrier, axial=axial - 2))
    if paired:
        when(both(under_hub, first), lambda: tell(barrier, axial=axial - 1, pitch=pitch + 1))
        when(both(even, has_up, first), lambda: tell(barrier, axial=axial - 2, pitch=pitch + 1))
    when(has_right, lambda: tell(barrier, span=span + 1))
    when(both(last_even, has_left), lambda: tell(barrier, span=span - 1))
    for other in range(npitch - 1):
        when(other < pitch, lambda: tell(barrier, pitch=jnp.int32(other)))
    for copy in state_copies:
        copy.start()

    heard = count(has_left, both(last_even, has_right), has_up, both(last_even, has_down))
    heard = heard + count(hub, hub) * (2 if paired else 1) + (npitch - 1 - pitch)
    pl.semaphore_wait(barrier, heard)

    when(both(under_hub, first), lambda: tell(even_ready, axial=axial - 1))
    when(hub, lambda: tell(odd_ready, axial=axial + 1))
    if paired:
        when(hub, lambda: tell(odd_ready, axial=axial + 1, pitch=pitch - 1))
    when(both(has_left, no(last_even)), lambda: tell(span_ready, span=span - 1))
    for other in range(1, npitch):
        when(other > pitch, lambda: tell(pitch_ready, pitch=jnp.int32(other)))

    def remote(src, dst, slot, **where):
        return pltpu.make_async_remote_copy(
            src_ref=src,
            dst_ref=dst,
            send_sem=send_sem.at[slot],
            recv_sem=recv_sem.at[slot],
            device_id=where,
            device_id_type=MESH,
        )

    down_copy = remote(
        state_hbm.at[:, :, rows - 4 :, :], ax_got.at[:, :, :4, :], 0, axial=axial + 1
    )
    up_copy = remote(state_hbm.at[:, :, :4, :], ax_got.at[:, :, 4:, :], 1, axial=axial - 1)
    right_copy = remote(sp_own, got_left, 2, span=span + 1)
    left_copy = remote(sp_own, got_right, 3, span=span - 1)

    when(has_up, up_copy.start)
    when(both(has_down, no(odd), no(both(hub_block, first))), down_copy.start)
    coef_copy.start()
    for copy in small_copies:
        copy.start()

    row = lax.broadcasted_iota(jnp.int32, (8, 128), 0)
    lane = lax.broadcasted_iota(jnp.int32, (8, 128), 1)
    group = lane // 8
    low_rows = row < 4

    half = cells // (sp_own.shape[1])

    def pack_span(f, carry):
        for g in range(sp_own.shape[1]):
            packed = jnp.zeros((8, 128), jnp.float32)
            for k in range(16):
                tile = u[f, g * half + k // tiles, (k % tiles) * 8 : (k % tiles) * 8 + 8, :]
                packed = jnp.where(group == k, pltpu.roll(tile, (8 * k + 4) % 128, 1), packed)
            sp_own[f, g] = packed
        return carry

    for f in range(fields):
        state_copies[f].wait()
        pack_span(f, 0)
    when(has_left, left_copy.start)
    when(both(has_right, last_even), right_copy.start)

    def flux_tile(t, carry):
        at = pl.ds(pl.multiple_of(t * 8, 8), 8)
        parts = [None] * 4
        for i in range(cells):
            cell = [u[f, i, at, :] for f in range(fields)]
            inverse = 1.0 / cell[0]
            speed = cell[2] * inverse
            kinetic = 0.5 * (cell[1] * cell[1] + cell[2] * cell[2] + cell[3] * cell[3]) * inverse
            pressure = (HEAT_RATIO_GAS - 1.0) * (cell[4] - kinetic)
            values = [
                cell[2],
                cell[1] * speed,
                cell[2] * speed + pressure,
                cell[3] * speed,
                (cell[4] + pressure) * speed,
            ]
            for f in range(fields):
                flux[f, i, at, :] = values[f]
            if i == 0:
                parts = [list(values), list(values), list(cell), list(cell)]
            else:
                for f in range(fields):
                    parts[0][f] = r * parts[0][f] + values[f]
                    parts[1][f] = parts[1][f] + (r**i) * values[f]
                    parts[2][f] = q * parts[2][f] + cell[f]
                    parts[3][f] = parts[3][f] + (q**i) * cell[f]
        for s in range(4):
            for f in range(fields):
                sums[s, f, at, :] = parts[s][f]
        return carry

    lax.fori_loop(0, tiles, flux_tile, 0, unroll=True)

    sum_copies = [
        remote(sums, got_sums.at[step - 1], 3 + step, pitch=lax.rem(pitch + step, npitch))
        for step in range(1, npitch)
    ]
    when(pitch > 0, lambda: pl.semaphore_wait(pitch_ready, pitch))
    for copy in sum_copies:
        copy.start()

    def clear(ref):
        ref[...] = jnp.zeros_like(ref)

    when(no(has_up), lambda: clear(ax_got.at[:, :, :4, :]))
    when(no(has_down), lambda: clear(ax_got.at[:, :, 4:, :]))
    when(no(has_left), lambda: clear(got_left))
    when(no(has_right), lambda: clear(got_right))

    weight = -DAMPING / 256.0

    def damp_field(f, carry):
        for i in range(cells):
            x = u[f, i]
            result = (140.0 * weight) * x
            for o, c in ((1, -56.0), (2, 28.0), (3, -8.0), (4, 1.0)):
                pair = (pltpu.roll(x, o, 0) + pltpu.roll(x, rows - o, 0)) + (
                    pltpu.roll(x, o, 1) + pltpu.roll(x, 128 - o, 1)
                )
                result = result + (c * weight) * pair
            out_ref[f, i] = result
            ends = jnp.where(low_rows, x[:8, :], x[rows - 8 :, :])
            ax_own[f, i] = -pltpu.roll(ends, 4, 0)
        return carry

    damp_field(0, 0)

    @pl.when(under_hub)
    def _():
        pl.semaphore_wait(odd_ready, 1)
        down_copy.start()

    @pl.when(both(hub_block, first))
    def _():
        pl.semaphore_wait(even_ready, 1)
        down_copy.start()

    damp_field(1, 0)

    @pl.when(both(has_right, no(last_even)))
    def _():
        pl.semaphore_wait(span_ready, 1)
        right_copy.start()

    for f in range(2, fields):
        damp_field(f, 0)

    for copy in small_copies:
        copy.wait()
    order = row.astype(jnp.float32) + 1.0
    phase = (2.0 * math.pi / PERIOD_SAMPLES) * order * lag_ref[0].astype(jnp.float32)
    active = row < harm_ref[...]
    waves[0] = jnp.where(active, jnp.cos(phase), 0.0)
    waves[1] = jnp.where(active, jnp.sin(phase), 0.0)
    near_first = pick(pitch, [r ** (cells * p) for p in range(npitch)])
    near_last = pick(pitch, [r ** (cells * (npitch - 1 - p)) for p in range(npitch)])
    jump_scale = -STEP_RATE * 0.75 * r_scale / (1.0 - r**total)
    jump_weights = [
        near_first * (jump_scale * (r**i + r ** (i + 1)))
        + near_last * (jump_scale * (r ** (cells - i) + r ** (cells - 1 - i)))
        for i in range(cells)
    ]
    flux_scale = -STEP_RATE * 0.75 * r_scale * (r - 1.0 / r)

    coef_copy.wait()

    def solve_field(f, carry):
        for t in range(tiles):
            at = pl.ds(t * 8, 8)
            jump = None
            for part in range(2):
                for k in range(harm_max):
                    term = waves[part, pl.ds(k, 1), :] * co[part, k, f, at, :]
                    jump = term if jump is None else jump + term
            x = [u[f, i, at, :] for i in range(cells)]
            y = [flux[f, i, at, :] for i in range(cells)]
            back_x, back_y = [None] * cells, [None] * cells
            carry_x, carry_y = q * x[cells - 1], y[cells - 1]
            for i in reversed(range(cells - 1)):
                back_x[i], back_y[i] = carry_x, carry_y
                if i > 0:
                    carry_x = q * (x[i] + carry_x)
                    carry_y = y[i] + r * carry_y
            front_x, front_y = None, None
            for i in range(cells):
                front_x = x[i] if front_x is None else x[i] + q * front_x
                value = out_ref[f, i, at, :] + jump_weights[i] * jump
                relaxed = front_x if back_x[i] is None else front_x + back_x[i]
                value = value + q_scale * relaxed
                slope = front_y
                if back_y[i] is not None:
                    slope = -back_y[i] if slope is None else slope - back_y[i]
                value = value + (flux_scale * r) * slope
                front_y = y[i] if front_y is None else y[i] + r * front_y
                out_ref[f, i, at, :] = value
        return carry

    lax.fori_loop(0, fields, solve_field, 0, unroll=True)

    for copy in sum_copies:
        copy.wait_recv()
    r_wrap = 1.0 / (1.0 - r**total)
    q_wrap = 1.0 / (1.0 - q**total)

    def carry_field(f, carry):
        for t in range(tiles):
            at = pl.ds(t * 8, 8)
            joined = []
            for s, (root, wrap) in enumerate(
                ((r, r_wrap), (r, r_wrap), (q, q_wrap), (q, q_wrap))
            ):
                value = (wrap * root ** (cells * (npitch - 1))) * sums[s, f, at, :]
                for step in range(1, npitch):
                    distance = step - 1 if s % 2 == 0 else npitch - 1 - step
                    factor = wrap * root ** (cells * distance)
                    value = value + factor * got_sums[step - 1, s, f, at, :]
                joined.append(value)
            for i in range(cells):
                out_ref[f, i, at, :] = (
                    out_ref[f, i, at, :]
                    + (flux_scale * r ** (i + 1)) * joined[0]
                    - (flux_scale * r ** (cells - i)) * joined[1]
                    + (q_scale * q ** (i + 1)) * joined[2]
                    + (q_scale * q ** (cells - i)) * joined[3]
                )
        return carry

    lax.fori_loop(0, fields, carry_field, 0, unroll=True)

    when(has_left, right_copy.wait_recv)
    when(has_right, left_copy.wait_recv)
    place = lane % 8
    outer = jnp.logical_or(lane < 4, lane >= 124)

    def span_field(f, carry):
        for g in range(sp_own.shape[1]):
            delta = jnp.where(place < 4, got_left[f, g], got_right[f, g]) - sp_own[f, g]
            ends = jnp.zeros((8, 128), jnp.float32)
            for t in range(4):
                ends = ends + jnp.where(
                    jnp.logical_and(place >= 4, place + t < 8),
                    EDGE[t] * weight,
                    0.0,
                ) * pltpu.roll(delta, 4 - t, 1)
                ends = ends + jnp.where(
                    jnp.logical_and(place < 4, place >= t),
                    EDGE[t] * weight,
                    0.0,
                ) * pltpu.roll(delta, 124 + t, 1)
            for k in range(16):
                i, t = g * half + k // tiles, k % tiles
                moved = pltpu.roll(ends, (124 - 8 * k) % 128, 1)
                out_ref[f, i, t * 8 : t * 8 + 8, :] += jnp.where(outer, moved, 0.0)
        return carry

    lax.fori_loop(0, fields, span_field, 0, unroll=True)

    when(has_up, down_copy.wait_recv)
    when(has_down, up_copy.wait_recv)
    near_low = [jnp.where(row + t < 4, EDGE[t] * weight, 0.0) for t in range(1, 4)]
    near_high = [jnp.where(row >= 4 + t, EDGE[t] * weight, 0.0) for t in range(1, 4)]

    def axial_field(f, carry):
        for i in range(cells):
            delta = ax_got[f, i] + ax_own[f, i]
            ends = (EDGE[0] * weight) * delta
            for t in range(1, 4):
                ends = ends + near_low[t - 1] * pltpu.roll(delta, 8 - t, 0)
                ends = ends + near_high[t - 1] * pltpu.roll(delta, t, 0)
            out_ref[f, i, :8, :] += jnp.where(low_rows, ends, 0.0)
            out_ref[f, i, rows - 8 :, :] += jnp.where(low_rows, 0.0, ends)
        return carry

    lax.fori_loop(0, fields, axial_field, 0, unroll=True)

    for copy in sum_copies:
        copy.wait_send()
    when(has_down, down_copy.wait_send)
    when(has_up, up_copy.wait_send)
    when(has_right, right_copy.wait_send)
    when(has_left, left_copy.wait_send)


def shards(sizes, state, coeffs, lag_shift, harmonics):
    fields, cells, rows, lanes = state.shape
    npitch = sizes[0]
    groups = cells * (rows // 8) // 16
    vmem = lambda *shape: pltpu.VMEM(shape, jnp.float32)
    halo = (fields, cells, 8, lanes)
    packed = (fields, groups, 8, lanes)
    sems = 4 + npitch - 1
    return pl.pallas_call(
        functools.partial(kernel, sizes),
        out_shape=pltpu.VMEM(state.shape, jnp.float32),
        in_specs=[
            pl.BlockSpec(memory_space=pltpu.HBM),
            pl.BlockSpec(memory_space=pltpu.HBM),
            pl.BlockSpec(memory_space=pltpu.HBM),
            pl.BlockSpec(memory_space=pltpu.HBM),
        ],
        out_specs=pl.BlockSpec(memory_space=pltpu.VMEM),
        scratch_shapes=[
            vmem(*state.shape),
            vmem(*coeffs.shape),
            vmem(*state.shape),
            vmem(4, fields, rows, lanes),
            vmem(npitch - 1, 4, fields, rows, lanes),
            vmem(*halo),
            vmem(*halo),
            vmem(*packed),
            vmem(*packed),
            vmem(*packed),
            vmem(2, 8, lanes),
            pltpu.SMEM((1,), jnp.int32),
            pltpu.VMEM((1, lanes), jnp.int32),
            pltpu.SemaphoreType.REGULAR,
            pltpu.SemaphoreType.REGULAR,
            pltpu.SemaphoreType.REGULAR,
            pltpu.SemaphoreType.REGULAR,
            pltpu.SemaphoreType.DMA((3 + fields,)),
            pltpu.SemaphoreType.DMA((sems,)),
            pltpu.SemaphoreType.DMA((sems,)),
        ],
        compiler_params=pltpu.CompilerParams(collective_id=0, has_side_effects=True),
    )(lag_shift, harmonics.reshape(1, lanes), state, coeffs)


def solution(mesh):
    sizes = tuple(mesh.shape[name] for name in ("pitch", "axial", "span"))
    placed = (
        P(None, "pitch", "axial", "span"),
        P(None, None, None, "axial", "span"),
        P(),
        P("span"),
    )
    return jax.shard_map(
        functools.partial(shards, sizes),
        mesh=mesh,
        in_specs=placed,
        out_specs=P(None, "pitch", "axial", "span"),
        check_vma=False,
    )
```

```python
import functools
import math

import jax
import jax.numpy as jnp
from jax import lax
from jax.experimental import pallas as pl
from jax.experimental.pallas import tpu as pltpu
from jax.sharding import PartitionSpec as P

PERIOD_SAMPLES = 64
HEAT_RATIO_GAS = 1.4
STEP_RATE = 0.25
DAMPING = 0.5
EDGE = (1.0, -8.0, 28.0, -56.0)
MESH = pl.DeviceIdType.MESH


def line_root(main, side):
    root = (-main + math.sqrt(main * main - 4.0 * side * side)) / (2.0 * side)
    return root, 1.0 / (main + 2.0 * side * root)


def pick(position, values):
    chosen = jnp.float32(values[-1])
    for index in range(len(values) - 1):
        chosen = jnp.where(position == index, jnp.float32(values[index]), chosen)
    return chosen


def kernel(
    sizes,
    lag_hbm,
    harm_hbm,
    state_hbm,
    coef_hbm,
    out_ref,
    u,
    co,
    flux,
    sums,
    got_sums,
    ax_own,
    ax_got,
    sp_left,
    sp_right,
    got_left,
    got_right,
    waves,
    lag_ref,
    harm_ref,
    pitch_ready,
    span_ready,
    odd_ready,
    even_ready,
    local_sem,
    send_sem,
    recv_sem,
):
    npitch, naxial, nspan = sizes
    fields, cells, rows, _ = u.shape
    tiles = rows // 8
    harm_max = co.shape[1]
    total = cells * npitch
    diffusion = float(total * total // 64)
    r, r_scale = line_root(1.0, 0.25)
    q, q_scale = line_root(1.0 + 2.0 * diffusion, -diffusion)
    pitch, axial, span = (lax.axis_index(name) for name in ("pitch", "axial", "span"))

    state_copies = [
        pltpu.make_async_copy(state_hbm.at[f], u.at[f], local_sem.at[3 + f]) for f in range(fields)
    ]
    coef_copy = pltpu.make_async_copy(coef_hbm, co, local_sem.at[0])
    small_copies = [
        pltpu.make_async_copy(lag_hbm, lag_ref, local_sem.at[1]),
        pltpu.make_async_copy(harm_hbm, harm_ref, local_sem.at[2]),
    ]

    def when(flag, action):
        @pl.when(flag)
        def _():
            action()

    def both(*flags):
        return functools.reduce(jnp.logical_and, flags)

    def no(flag):
        return jnp.logical_not(flag)

    paired = npitch % 2 == 0
    has_up, has_down = axial > 0, axial < naxial - 1
    has_left, has_right = span > 0, span < nspan - 1
    odd = lax.rem(axial, 2) == 1
    even = no(odd)
    hub_block = both(even, axial + 2 < naxial)
    last_even = both(even, axial + 2 >= naxial)
    second = lax.rem(pitch, 2) == 1 if paired else pitch >= 0
    first = no(second)
    hub = both(hub_block, second)
    under_hub = both(odd, has_down)

    barrier = pltpu.get_barrier_semaphore()

    def tell(semaphore, **where):
        pl.semaphore_signal(semaphore, inc=1, device_id=where, device_id_type=MESH)

    def count(*flags):
        return sum(jnp.where(flag, 1, 0) for flag in flags)

    when(both(odd, no(both(has_down, first))), lambda: tell(barrier, axial=axial - 1))
    when(under_hub, lambda: tell(barrier, axial=axial + 1))
    when(both(even, has_down), lambda: tell(barrier, axial=axial + 1))
    when(both(even, has_up, second), lambda: tell(barrier, axial=axial - 2))
    if paired:
        when(both(under_hub, first), lambda: tell(barrier, axial=axial - 1, pitch=pitch + 1))
        when(both(even, has_up, first), lambda: tell(barrier, axial=axial - 2, pitch=pitch + 1))
    when(has_right, lambda: tell(barrier, span=span + 1))
    when(both(last_even, has_left), lambda: tell(barrier, span=span - 1))
    for other in range(npitch - 1):
        when(other < pitch, lambda: tell(barrier, pitch=jnp.int32(other)))
    for copy in state_copies:
        copy.start()

    heard = count(has_left, both(last_even, has_right), has_up, both(last_even, has_down))
    heard = heard + count(hub, hub) * (2 if paired else 1) + (npitch - 1 - pitch)
    pl.semaphore_wait(barrier, heard)

    when(both(under_hub, first), lambda: tell(even_ready, axial=axial - 1))
    when(hub, lambda: tell(odd_ready, axial=axial + 1))
    if paired:
        when(hub, lambda: tell(odd_ready, axial=axial + 1, pitch=pitch - 1))
    when(both(has_left, no(last_even)), lambda: tell(span_ready, span=span - 1))
    for other in range(1, npitch):
        when(other > pitch, lambda: tell(pitch_ready, pitch=jnp.int32(other)))

    def remote(src, dst, slot, **where):
        return pltpu.make_async_remote_copy(
            src_ref=src,
            dst_ref=dst,
            send_sem=send_sem.at[slot],
            recv_sem=recv_sem.at[slot],
            device_id=where,
            device_id_type=MESH,
        )

    down_copy = remote(u.at[:, :, rows - 4 :, :], ax_got.at[:, :, :4, :], 0, axial=axial + 1)
    up_copy = remote(u.at[:, :, :4, :], ax_got.at[:, :, 4:, :], 1, axial=axial - 1)
    soon_copy = remote(state_hbm.at[:, :, :4, :], ax_got.at[:, :, 4:, :], 1, axial=axial - 1)
    right_copy = remote(sp_right, got_left, 2, span=span + 1)
    left_copy = remote(sp_left, got_right, 3, span=span - 1)

    when(odd, soon_copy.start)
    coef_copy.start()
    for copy in small_copies:
        copy.start()

    row = lax.broadcasted_iota(jnp.int32, (8, 128), 0)
    lane = lax.broadcasted_iota(jnp.int32, (8, 128), 1)
    group, place = lane // 4, lane % 4
    low_rows = row < 4

    for copy in state_copies:
        copy.wait()
    when(both(has_up, even), up_copy.start)
    when(both(has_down, even, no(both(hub_block, first))), down_copy.start)

    groups = sp_left.shape[1]

    def pack_span(f, carry):
        for g in range(groups):
            right = left = jnp.zeros((8, 128), jnp.float32)
            for k in range(32):
                i, t = divmod(g * 32 + k, tiles)
                moved = pltpu.roll(u[f, i, t * 8 : t * 8 + 8, :], (4 * k + 4) % 128, 1)
                right = jnp.where(group == k, moved, right)
                left = jnp.where(group == (k + 1) % 32, moved, left)
            sp_right[f, g] = right
            sp_left[f, g] = left
        return carry

    for f in range(fields):
        pack_span(f, 0)
    when(has_left, left_copy.start)
    when(both(has_right, last_even), right_copy.start)

    def flux_tile(t, carry):
        at = pl.ds(pl.multiple_of(t * 8, 8), 8)
        parts = [None] * 4
        for i in range(cells):
            cell = [u[f, i, at, :] for f in range(fields)]
            inverse = 1.0 / cell[0]
            speed = cell[2] * inverse
            kinetic = 0.5 * (cell[1] * cell[1] + cell[2] * cell[2] + cell[3] * cell[3]) * inverse
            pressure = (HEAT_RATIO_GAS - 1.0) * (cell[4] - kinetic)
            values = [
                cell[2],
                cell[1] * speed,
                cell[2] * speed + pressure,
                cell[3] * speed,
                (cell[4] + pressure) * speed,
            ]
            for f in range(fields):
                flux[f, i, at, :] = values[f]
            if i == 0:
                parts = [list(values), list(values), list(cell), list(cell)]
            else:
                for f in range(fields):
                    parts[0][f] = r * parts[0][f] + values[f]
                    parts[1][f] = parts[1][f] + (r**i) * values[f]
                    parts[2][f] = q * parts[2][f] + cell[f]
                    parts[3][f] = parts[3][f] + (q**i) * cell[f]
        for s in range(4):
            for f in range(fields):
                sums[s, f, at, :] = parts[s][f]
        return carry

    lax.fori_loop(0, tiles, flux_tile, 0, unroll=True)

    sum_copies = [
        remote(sums, got_sums.at[step - 1], 3 + step, pitch=lax.rem(pitch + step, npitch))
        for step in range(1, npitch)
    ]
    when(pitch > 0, lambda: pl.semaphore_wait(pitch_ready, pitch))
    for copy in sum_copies:
        copy.start()

    def clear(ref):
        ref[...] = jnp.zeros_like(ref)

    when(no(has_up), lambda: clear(ax_got.at[:, :, :4, :]))
    when(no(has_down), lambda: clear(ax_got.at[:, :, 4:, :]))
    when(no(has_left), lambda: clear(got_left))
    when(no(has_right), lambda: clear(got_right))

    weight = -DAMPING / 256.0

    def damp_field(f, carry):
        for i in range(cells):
            x = u[f, i]
            result = (140.0 * weight) * x
            for o, c in ((1, -56.0), (2, 28.0), (3, -8.0), (4, 1.0)):
                pair = (pltpu.roll(x, o, 0) + pltpu.roll(x, rows - o, 0)) + (
                    pltpu.roll(x, o, 1) + pltpu.roll(x, 128 - o, 1)
                )
                result = result + (c * weight) * pair
            out_ref[f, i] = result
            ends = jnp.where(low_rows, x[:8, :], x[rows - 8 :, :])
            ax_own[f, i] = -pltpu.roll(ends, 4, 0)
        return carry

    damp_field(0, 0)

    @pl.when(under_hub)
    def _():
        pl.semaphore_wait(odd_ready, 1)
        down_copy.start()

    @pl.when(both(hub_block, first))
    def _():
        pl.semaphore_wait(even_ready, 1)
        down_copy.start()

    damp_field(1, 0)

    @pl.when(both(has_right, no(last_even)))
    def _():
        pl.semaphore_wait(span_ready, 1)
        right_copy.start()

    for f in range(2, fields):
        damp_field(f, 0)

    for copy in small_copies:
        copy.wait()
    order = row.astype(jnp.float32) + 1.0
    phase = (2.0 * math.pi / PERIOD_SAMPLES) * order * lag_ref[0].astype(jnp.float32)
    active = row < harm_ref[...]
    waves[0] = jnp.where(active, jnp.cos(phase), 0.0)
    waves[1] = jnp.where(active, jnp.sin(phase), 0.0)
    near_first = pick(pitch, [r ** (cells * p) for p in range(npitch)])
    near_last = pick(pitch, [r ** (cells * (npitch - 1 - p)) for p in range(npitch)])
    jump_scale = -STEP_RATE * 0.75 * r_scale / (1.0 - r**total)
    jump_weights = [
        near_first * (jump_scale * (r**i + r ** (i + 1)))
        + near_last * (jump_scale * (r ** (cells - i) + r ** (cells - 1 - i)))
        for i in range(cells)
    ]
    flux_scale = -STEP_RATE * 0.75 * r_scale * (r - 1.0 / r)

    coef_copy.wait()

    def solve_field(f, carry):
        for t in range(tiles):
            at = pl.ds(t * 8, 8)
            jump = None
            for part in range(2):
                for k in range(harm_max):
                    term = waves[part, pl.ds(k, 1), :] * co[part, k, f, at, :]
                    jump = term if jump is None else jump + term
            x = [u[f, i, at, :] for i in range(cells)]
            y = [flux[f, i, at, :] for i in range(cells)]
            back_x, back_y = [None] * cells, [None] * cells
            carry_x, carry_y = q * x[cells - 1], y[cells - 1]
            for i in reversed(range(cells - 1)):
                back_x[i], back_y[i] = carry_x, carry_y
                if i > 0:
                    carry_x = q * (x[i] + carry_x)
                    carry_y = y[i] + r * carry_y
            front_x, front_y = None, None
            for i in range(cells):
                front_x = x[i] if front_x is None else x[i] + q * front_x
                value = out_ref[f, i, at, :] + jump_weights[i] * jump
                relaxed = front_x if back_x[i] is None else front_x + back_x[i]
                value = value + q_scale * relaxed
                slope = front_y
                if back_y[i] is not None:
                    slope = -back_y[i] if slope is None else slope - back_y[i]
                value = value + (flux_scale * r) * slope
                front_y = y[i] if front_y is None else y[i] + r * front_y
                out_ref[f, i, at, :] = value
        return carry

    lax.fori_loop(0, fields, solve_field, 0, unroll=True)

    for copy in sum_copies:
        copy.wait_recv()
    r_wrap = 1.0 / (1.0 - r**total)
    q_wrap = 1.0 / (1.0 - q**total)

    def carry_field(f, carry):
        for t in range(tiles):
            at = pl.ds(t * 8, 8)
            joined = []
            for s, (root, wrap) in enumerate(
                ((r, r_wrap), (r, r_wrap), (q, q_wrap), (q, q_wrap))
            ):
                value = (wrap * root ** (cells * (npitch - 1))) * sums[s, f, at, :]
                for step in range(1, npitch):
                    distance = step - 1 if s % 2 == 0 else npitch - 1 - step
                    factor = wrap * root ** (cells * distance)
                    value = value + factor * got_sums[step - 1, s, f, at, :]
                joined.append(value)
            for i in range(cells):
                out_ref[f, i, at, :] = (
                    out_ref[f, i, at, :]
                    + (flux_scale * r ** (i + 1)) * joined[0]
                    - (flux_scale * r ** (cells - i)) * joined[1]
                    + (q_scale * q ** (i + 1)) * joined[2]
                    + (q_scale * q ** (cells - i)) * joined[3]
                )
        return carry

    lax.fori_loop(0, fields, carry_field, 0, unroll=True)

    when(has_left, right_copy.wait_recv)
    when(has_right, left_copy.wait_recv)
    outer = jnp.logical_or(lane < 4, lane >= 124)
    from_left = [jnp.where(place + t < 4, EDGE[t] * weight, 0.0) for t in range(4)]
    from_right = [jnp.where(place >= t, EDGE[t] * weight, 0.0) for t in range(4)]
    even_group = group % 2 == 0

    def span_field(f, carry):
        for g in range(groups):
            before = got_left[f, g] - sp_right[f, g]
            after = got_right[f, g] - sp_left[f, g]
            starts, stops = from_left[0] * before, from_right[0] * after
            for t in range(1, 4):
                starts = starts + from_left[t] * pltpu.roll(before, 128 - t, 1)
                stops = stops + from_right[t] * pltpu.roll(after, t, 1)
            stops = pltpu.roll(stops, 120, 1)
            ends = (
                jnp.where(even_group, starts, stops),
                jnp.where(even_group, stops, starts),
            )
            for k in range(32):
                i, t = divmod(g * 32 + k, tiles)
                moved = pltpu.roll(ends[k % 2], (128 - 4 * k) % 128, 1)
                out_ref[f, i, t * 8 : t * 8 + 8, :] += jnp.where(outer, moved, 0.0)
        return carry

    lax.fori_loop(0, fields, span_field, 0, unroll=True)

    when(has_up, down_copy.wait_recv)
    when(has_down, up_copy.wait_recv)
    near_low = [jnp.where(row + t < 4, EDGE[t] * weight, 0.0) for t in range(1, 4)]
    near_high = [jnp.where(row >= 4 + t, EDGE[t] * weight, 0.0) for t in range(1, 4)]

    def axial_field(f, carry):
        for i in range(cells):
            delta = ax_got[f, i] + ax_own[f, i]
            ends = (EDGE[0] * weight) * delta
            for t in range(1, 4):
                ends = ends + near_low[t - 1] * pltpu.roll(delta, 8 - t, 0)
                ends = ends + near_high[t - 1] * pltpu.roll(delta, t, 0)
            out_ref[f, i, :8, :] += jnp.where(low_rows, ends, 0.0)
            out_ref[f, i, rows - 8 :, :] += jnp.where(low_rows, 0.0, ends)
        return carry

    lax.fori_loop(0, fields, axial_field, 0, unroll=True)

    for copy in sum_copies:
        copy.wait_send()
    when(has_down, down_copy.wait_send)
    when(has_up, up_copy.wait_send)
    when(has_right, right_copy.wait_send)
    when(has_left, left_copy.wait_send)


def shards(sizes, state, coeffs, lag_shift, harmonics):
    fields, cells, rows, lanes = state.shape
    npitch = sizes[0]
    groups = cells * (rows // 8) // 32
    vmem = lambda *shape: pltpu.VMEM(shape, jnp.float32)
    halo = (fields, cells, 8, lanes)
    packed = (fields, groups, 8, lanes)
    sems = 4 + npitch - 1
    return pl.pallas_call(
        functools.partial(kernel, sizes),
        out_shape=pltpu.VMEM(state.shape, jnp.float32),
        in_specs=[
            pl.BlockSpec(memory_space=pltpu.HBM),
            pl.BlockSpec(memory_space=pltpu.HBM),
            pl.BlockSpec(memory_space=pltpu.HBM),
            pl.BlockSpec(memory_space=pltpu.HBM),
        ],
        out_specs=pl.BlockSpec(memory_space=pltpu.VMEM),
        scratch_shapes=[
            vmem(*state.shape),
            vmem(*coeffs.shape),
            vmem(*state.shape),
            vmem(4, fields, rows, lanes),
            vmem(npitch - 1, 4, fields, rows, lanes),
            vmem(*halo),
            vmem(*halo),
            vmem(*packed),
            vmem(*packed),
            vmem(*packed),
            vmem(*packed),
            vmem(2, 8, lanes),
            pltpu.SMEM((1,), jnp.int32),
            pltpu.VMEM((1, lanes), jnp.int32),
            pltpu.SemaphoreType.REGULAR,
            pltpu.SemaphoreType.REGULAR,
            pltpu.SemaphoreType.REGULAR,
            pltpu.SemaphoreType.REGULAR,
            pltpu.SemaphoreType.DMA((3 + fields,)),
            pltpu.SemaphoreType.DMA((sems,)),
            pltpu.SemaphoreType.DMA((sems,)),
        ],
        compiler_params=pltpu.CompilerParams(collective_id=0, has_side_effects=True),
    )(lag_shift, harmonics.reshape(1, lanes), state, coeffs)


def solution(mesh):
    sizes = tuple(mesh.shape[name] for name in ("pitch", "axial", "span"))
    placed = (
        P(None, "pitch", "axial", "span"),
        P(None, None, None, "axial", "span"),
        P(),
        P("span"),
    )
    return jax.shard_map(
        functools.partial(shards, sizes),
        mesh=mesh,
        in_specs=placed,
        out_specs=P(None, "pitch", "axial", "span"),
        check_vma=False,
    )
```

```python
import functools
import math

import jax
import jax.numpy as jnp
from jax import lax
from jax.experimental import pallas as pl
from jax.experimental.pallas import tpu as pltpu
from jax.sharding import PartitionSpec as P

PERIOD_SAMPLES = 64
HEAT_RATIO_GAS = 1.4
STEP_RATE = 0.25
DAMPING = 0.5
EDGE = (1.0, -8.0, 28.0, -56.0)
MESH = pl.DeviceIdType.MESH


def line_root(main, side):
    root = (-main + math.sqrt(main * main - 4.0 * side * side)) / (2.0 * side)
    return root, 1.0 / (main + 2.0 * side * root)


def split(fields):
    cuts = sorted({0, fields * 2 // 5, fields * 4 // 5, fields})
    return tuple(zip(cuts[:-1], cuts[1:]))


def pick(position, values):
    chosen = jnp.float32(values[-1])
    for index in range(len(values) - 1):
        chosen = jnp.where(position == index, jnp.float32(values[index]), chosen)
    return chosen


def kernel(
    sizes,
    lag_hbm,
    harm_hbm,
    state_hbm,
    coef_hbm,
    out_ref,
    u,
    co,
    flux,
    sums,
    got_sums,
    ax_own,
    ax_got,
    sp_left,
    sp_right,
    got_left,
    got_right,
    waves,
    lag_ref,
    harm_ref,
    pitch_ready,
    span_ready,
    next_ready,
    local_sem,
    send_sem,
    recv_sem,
):
    npitch, naxial, nspan = sizes
    fields, cells, rows, _ = u.shape
    tiles = rows // 8
    parts = split(fields)
    harm_max = co.shape[1]
    total = cells * npitch
    diffusion = float(total * total // 64)
    r, r_scale = line_root(1.0, 0.25)
    q, q_scale = line_root(1.0 + 2.0 * diffusion, -diffusion)
    pitch, axial, span = (lax.axis_index(name) for name in ("pitch", "axial", "span"))

    state_copy = pltpu.make_async_copy(state_hbm, u, local_sem.at[3])
    coef_copy = pltpu.make_async_copy(coef_hbm, co, local_sem.at[0])
    small_copies = [
        pltpu.make_async_copy(lag_hbm, lag_ref, local_sem.at[1]),
        pltpu.make_async_copy(harm_hbm, harm_ref, local_sem.at[2]),
    ]

    def when(flag, action):
        @pl.when(flag)
        def _():
            action()

    def both(*flags):
        return functools.reduce(jnp.logical_and, flags)

    def no(flag):
        return jnp.logical_not(flag)

    paired = npitch % 2 == 0
    has_up, has_down = axial > 0, axial < naxial - 1
    has_left, has_right = span > 0, span < nspan - 1
    odd = lax.rem(axial, 2) == 1
    even = no(odd)
    hub_block = both(even, axial + 2 < naxial)
    last_even = both(even, axial + 2 >= naxial)
    second = lax.rem(pitch, 2) == 1 if paired else pitch >= 0
    first = no(second)
    hub = both(hub_block, second)
    under_hub = both(odd, has_down)

    state_copy.start()
    barrier = pltpu.get_barrier_semaphore()

    def tell(semaphore, **where):
        pl.semaphore_signal(semaphore, inc=1, device_id=where, device_id_type=MESH)

    def count(*flags):
        return sum(jnp.where(flag, 1, 0) for flag in flags)

    heard_by = pitch
    if paired:
        heard_by = jnp.where(both(first, jnp.logical_or(even, has_down)), pitch + 1, pitch)
    when(
        has_up,
        lambda: tell(barrier, axial=jnp.where(odd, axial - 1, axial - 2), pitch=heard_by),
    )
    when(has_down, lambda: tell(barrier, axial=axial + 1))
    when(has_right, lambda: tell(barrier, span=span + 1))
    for other in range(npitch - 1):
        when(other < pitch, lambda: tell(barrier, pitch=jnp.int32(other)))

    heard = count(has_left, has_up, both(last_even, has_down))
    heard = heard + count(hub, hub) * (2 if paired else 1) + (npitch - 1 - pitch)
    pl.semaphore_wait(barrier, heard)

    def remote(src, dst, slot, **where):
        return pltpu.make_async_remote_copy(
            src_ref=src,
            dst_ref=dst,
            send_sem=send_sem.at[slot],
            recv_sem=recv_sem.at[slot],
            device_id=where,
            device_id_type=MESH,
        )

    def axial_part(src, from_row, to_row, slot, part, target):
        some = slice(*part)
        return remote(
            src.at[some, :, from_row : from_row + 4, :],
            ax_got.at[some, :, to_row : to_row + 4, :],
            slot,
            axial=target,
        )

    down_copies, up_copies, soon_copies = [], [], []
    for k, part in enumerate(parts):
        down_copies.append(axial_part(u, rows - 4, 0, 2 * k, part, axial + 1))
        up_copies.append(axial_part(u, 0, 4, 2 * k + 1, part, axial - 1))
        soon_copies.append(axial_part(state_hbm, 0, 4, 2 * k + 1, part, axial - 1))
    slots = 2 * len(parts)

    def start_all(copies):
        for copy in copies:
            copy.start()

    right_copy = remote(sp_right, got_left, slots, span=span + 1)
    left_copy = remote(sp_left, got_right, slots + 1, span=span - 1)

    when(odd, lambda: start_all(soon_copies))
    if paired:
        when(hub, lambda: tell(next_ready, axial=axial + 1, pitch=pitch - 1))
    when(hub, lambda: tell(next_ready, axial=axial + 1))
    when(both(under_hub, first), lambda: tell(next_ready, axial=axial - 1))
    when(has_left, lambda: tell(span_ready, span=span - 1))
    for other in range(1, npitch):
        when(other > pitch, lambda: tell(pitch_ready, pitch=jnp.int32(other)))
    row = lax.broadcasted_iota(jnp.int32, (8, 128), 0)
    lane = lax.broadcasted_iota(jnp.int32, (8, 128), 1)
    group, place = lane // 4, lane % 4
    low_rows = row < 4

    state_copy.wait()
    when(both(even, has_up), lambda: start_all(up_copies))
    when(both(has_down, even, no(both(hub_block, first))), lambda: start_all(down_copies))

    groups = sp_left.shape[1]

    def pack_span(f, carry):
        for g in range(groups):
            right = left = jnp.zeros((8, 128), jnp.float32)
            for k in range(32):
                i, t = divmod(g * 32 + k, tiles)
                moved = pltpu.roll(u[f, i, t * 8 : t * 8 + 8, :], (4 * k + 4) % 128, 1)
                right = jnp.where(group == k, moved, right)
                left = jnp.where(group == (k + 1) % 32, moved, left)
            sp_right[f, g] = right
            sp_left[f, g] = left
        return carry

    for f in range(fields):
        pack_span(f, 0)
    when(has_left, left_copy.start)
    coef_copy.start()
    for copy in small_copies:
        copy.start()

    def flux_tile(t, carry):
        at = pl.ds(pl.multiple_of(t * 8, 8), 8)
        parts = [None] * 4
        for i in range(cells):
            cell = [u[f, i, at, :] for f in range(fields)]
            inverse = 1.0 / cell[0]
            speed = cell[2] * inverse
            kinetic = 0.5 * (cell[1] * cell[1] + cell[2] * cell[2] + cell[3] * cell[3]) * inverse
            pressure = (HEAT_RATIO_GAS - 1.0) * (cell[4] - kinetic)
            values = [
                cell[2],
                cell[1] * speed,
                cell[2] * speed + pressure,
                cell[3] * speed,
                (cell[4] + pressure) * speed,
            ]
            for f in range(fields):
                flux[f, i, at, :] = values[f]
            if i == 0:
                parts = [list(values), list(values), list(cell), list(cell)]
            else:
                for f in range(fields):
                    parts[0][f] = r * parts[0][f] + values[f]
                    parts[1][f] = parts[1][f] + (r**i) * values[f]
                    parts[2][f] = q * parts[2][f] + cell[f]
                    parts[3][f] = parts[3][f] + (q**i) * cell[f]
        for s in range(4):
            for f in range(fields):
                sums[s, f, at, :] = parts[s][f]
        return carry

    lax.fori_loop(0, tiles, flux_tile, 0, unroll=True)

    sum_copies = [
        remote(sums, got_sums.at[step - 1], slots + 1 + step, pitch=lax.rem(pitch + step, npitch))
        for step in range(1, npitch)
    ]
    when(pitch > 0, lambda: pl.semaphore_wait(pitch_ready, pitch))
    for copy in sum_copies:
        copy.start()

    def clear(ref):
        ref[...] = jnp.zeros_like(ref)

    when(no(has_up), lambda: clear(ax_got.at[:, :, :4, :]))
    when(no(has_down), lambda: clear(ax_got.at[:, :, 4:, :]))
    when(no(has_left), lambda: clear(got_left))
    when(no(has_right), lambda: clear(got_right))

    weight = -DAMPING / 256.0

    def damp_field(f, carry):
        for i in range(cells):
            x = u[f, i]
            result = (140.0 * weight) * x
            for o, c in ((1, -56.0), (2, 28.0), (3, -8.0), (4, 1.0)):
                pair = (pltpu.roll(x, o, 0) + pltpu.roll(x, rows - o, 0)) + (
                    pltpu.roll(x, o, 1) + pltpu.roll(x, 128 - o, 1)
                )
                result = result + (c * weight) * pair
            out_ref[f, i] = result
            ends = jnp.where(low_rows, x[:8, :], x[rows - 8 :, :])
            ax_own[f, i] = -pltpu.roll(ends, 4, 0)
        return carry

    @pl.when(jnp.logical_or(under_hub, both(hub_block, first)))
    def _():
        pl.semaphore_wait(next_ready, 1)
        start_all(down_copies)

    damp_field(0, 0)
    damp_field(1, 0)

    @pl.when(has_right)
    def _():
        pl.semaphore_wait(span_ready, 1)
        right_copy.start()

    for f in range(2, fields):
        damp_field(f, 0)

    for copy in small_copies:
        copy.wait()
    order = row.astype(jnp.float32) + 1.0
    phase = (2.0 * math.pi / PERIOD_SAMPLES) * order * lag_ref[0].astype(jnp.float32)
    active = row < harm_ref[...]
    waves[0] = jnp.where(active, jnp.cos(phase), 0.0)
    waves[1] = jnp.where(active, jnp.sin(phase), 0.0)
    near_first = pick(pitch, [r ** (cells * p) for p in range(npitch)])
    near_last = pick(pitch, [r ** (cells * (npitch - 1 - p)) for p in range(npitch)])
    jump_scale = -STEP_RATE * 0.75 * r_scale / (1.0 - r**total)
    jump_weights = [
        near_first * (jump_scale * (r**i + r ** (i + 1)))
        + near_last * (jump_scale * (r ** (cells - i) + r ** (cells - 1 - i)))
        for i in range(cells)
    ]
    flux_scale = -STEP_RATE * 0.75 * r_scale * (r - 1.0 / r)

    coef_copy.wait()

    def solve_field(f, carry):
        for t in range(tiles):
            at = pl.ds(t * 8, 8)
            jump = None
            for part in range(2):
                for k in range(harm_max):
                    term = waves[part, pl.ds(k, 1), :] * co[part, k, f, at, :]
                    jump = term if jump is None else jump + term
            x = [u[f, i, at, :] for i in range(cells)]
            y = [flux[f, i, at, :] for i in range(cells)]
            back_x, back_y = [None] * cells, [None] * cells
            carry_x, carry_y = q * x[cells - 1], y[cells - 1]
            for i in reversed(range(cells - 1)):
                back_x[i], back_y[i] = carry_x, carry_y
                if i > 0:
                    carry_x = q * (x[i] + carry_x)
                    carry_y = y[i] + r * carry_y
            front_x, front_y = None, None
            for i in range(cells):
                front_x = x[i] if front_x is None else x[i] + q * front_x
                value = out_ref[f, i, at, :] + jump_weights[i] * jump
                relaxed = front_x if back_x[i] is None else front_x + back_x[i]
                value = value + q_scale * relaxed
                slope = front_y
                if back_y[i] is not None:
                    slope = -back_y[i] if slope is None else slope - back_y[i]
                value = value + (flux_scale * r) * slope
                front_y = y[i] if front_y is None else y[i] + r * front_y
                out_ref[f, i, at, :] = value
        return carry

    lax.fori_loop(0, fields, solve_field, 0, unroll=True)

    for copy in sum_copies:
        copy.wait_recv()
    r_wrap = 1.0 / (1.0 - r**total)
    q_wrap = 1.0 / (1.0 - q**total)

    def carry_field(f, carry):
        for t in range(tiles):
            at = pl.ds(t * 8, 8)
            joined = []
            for s, (root, wrap) in enumerate(
                ((r, r_wrap), (r, r_wrap), (q, q_wrap), (q, q_wrap))
            ):
                value = (wrap * root ** (cells * (npitch - 1))) * sums[s, f, at, :]
                for step in range(1, npitch):
                    distance = step - 1 if s % 2 == 0 else npitch - 1 - step
                    factor = wrap * root ** (cells * distance)
                    value = value + factor * got_sums[step - 1, s, f, at, :]
                joined.append(value)
            for i in range(cells):
                out_ref[f, i, at, :] = (
                    out_ref[f, i, at, :]
                    + (flux_scale * r ** (i + 1)) * joined[0]
                    - (flux_scale * r ** (cells - i)) * joined[1]
                    + (q_scale * q ** (i + 1)) * joined[2]
                    + (q_scale * q ** (cells - i)) * joined[3]
                )
        return carry

    lax.fori_loop(0, fields, carry_field, 0, unroll=True)

    outer = jnp.logical_or(lane < 4, lane >= 124)
    from_left = [jnp.where(place + t < 4, EDGE[t] * weight, 0.0) for t in range(4)]
    from_right = [jnp.where(place >= t, EDGE[t] * weight, 0.0) for t in range(4)]
    even_group = group % 2 == 0

    def span_field(f, carry):
        for g in range(groups):
            before = got_left[f, g] - sp_right[f, g]
            after = got_right[f, g] - sp_left[f, g]
            starts, stops = from_left[0] * before, from_right[0] * after
            for t in range(1, 4):
                starts = starts + from_left[t] * pltpu.roll(before, 128 - t, 1)
                stops = stops + from_right[t] * pltpu.roll(after, t, 1)
            stops = pltpu.roll(stops, 120, 1)
            ends = (
                jnp.where(even_group, starts, stops),
                jnp.where(even_group, stops, starts),
            )
            for k in range(32):
                i, t = divmod(g * 32 + k, tiles)
                moved = pltpu.roll(ends[k % 2], (128 - 4 * k) % 128, 1)
                out_ref[f, i, t * 8 : t * 8 + 8, :] += jnp.where(outer, moved, 0.0)
        return carry

    def span_ends():
        when(has_left, right_copy.wait_recv)
        when(has_right, left_copy.wait_recv)
        lax.fori_loop(0, fields, span_field, 0, unroll=True)

    corner = both(axial == 0, span == 0)
    when(no(corner), span_ends)

    near_low = [jnp.where(row + t < 4, EDGE[t] * weight, 0.0) for t in range(1, 4)]
    near_high = [jnp.where(row >= 4 + t, EDGE[t] * weight, 0.0) for t in range(1, 4)]

    def axial_field(f, carry):
        for i in range(cells):
            delta = ax_got[f, i] + ax_own[f, i]
            ends = (EDGE[0] * weight) * delta
            for t in range(1, 4):
                ends = ends + near_low[t - 1] * pltpu.roll(delta, 8 - t, 0)
                ends = ends + near_high[t - 1] * pltpu.roll(delta, t, 0)
            out_ref[f, i, :8, :] += jnp.where(low_rows, ends, 0.0)
            out_ref[f, i, rows - 8 :, :] += jnp.where(low_rows, 0.0, ends)
        return carry

    for k, part in enumerate(parts):
        when(has_up, down_copies[k].wait_recv)
        when(has_down, up_copies[k].wait_recv)
        for f in range(*part):
            axial_field(f, 0)
    when(corner, span_ends)

    for copy in sum_copies:
        copy.wait_send()
    for k in range(len(parts)):
        when(has_down, down_copies[k].wait_send)
        when(has_up, up_copies[k].wait_send)
    when(has_right, right_copy.wait_send)
    when(has_left, left_copy.wait_send)


def shards(sizes, state, coeffs, lag_shift, harmonics):
    fields, cells, rows, lanes = state.shape
    npitch = sizes[0]
    groups = cells * (rows // 8) // 32
    vmem = lambda *shape: pltpu.VMEM(shape, jnp.float32)
    halo = (fields, cells, 8, lanes)
    packed = (fields, groups, 8, lanes)
    sems = 2 * len(split(fields)) + 2 + npitch - 1
    return pl.pallas_call(
        functools.partial(kernel, sizes),
        out_shape=pltpu.VMEM(state.shape, jnp.float32),
        in_specs=[
            pl.BlockSpec(memory_space=pltpu.HBM),
            pl.BlockSpec(memory_space=pltpu.HBM),
            pl.BlockSpec(memory_space=pltpu.HBM),
            pl.BlockSpec(memory_space=pltpu.HBM),
        ],
        out_specs=pl.BlockSpec(memory_space=pltpu.VMEM),
        scratch_shapes=[
            vmem(*state.shape),
            vmem(*coeffs.shape),
            vmem(*state.shape),
            vmem(4, fields, rows, lanes),
            vmem(npitch - 1, 4, fields, rows, lanes),
            vmem(*halo),
            vmem(*halo),
            vmem(*packed),
            vmem(*packed),
            vmem(*packed),
            vmem(*packed),
            vmem(2, 8, lanes),
            pltpu.SMEM((1,), jnp.int32),
            pltpu.VMEM((1, lanes), jnp.int32),
            pltpu.SemaphoreType.REGULAR,
            pltpu.SemaphoreType.REGULAR,
            pltpu.SemaphoreType.REGULAR,
            pltpu.SemaphoreType.DMA((4,)),
            pltpu.SemaphoreType.DMA((sems,)),
            pltpu.SemaphoreType.DMA((sems,)),
        ],
        compiler_params=pltpu.CompilerParams(collective_id=0, has_side_effects=True),
    )(lag_shift, harmonics.reshape(1, lanes), state, coeffs)


def solution(mesh):
    sizes = tuple(mesh.shape[name] for name in ("pitch", "axial", "span"))
    placed = (
        P(None, "pitch", "axial", "span"),
        P(None, None, None, "axial", "span"),
        P(),
        P("span"),
    )
    return jax.shard_map(
        functools.partial(shards, sizes),
        mesh=mesh,
        in_specs=placed,
        out_specs=P(None, "pitch", "axial", "span"),
        check_vma=False,
    )
```

```python
import functools
import math

import jax
import jax.numpy as jnp
from jax import lax
from jax.experimental import pallas as pl
from jax.experimental.pallas import tpu as pltpu
from jax.sharding import PartitionSpec as P

PERIOD_SAMPLES = 64
HEAT_RATIO_GAS = 1.4
STEP_RATE = 0.25
DAMPING = 0.5
EDGE = (1.0, -8.0, 28.0, -56.0)
MESH = pl.DeviceIdType.MESH
AXIAL_CUTS, SPAN_CUTS = (4,), (3,)


def line_root(main, side):
    root = (-main + math.sqrt(main * main - 4.0 * side * side)) / (2.0 * side)
    return root, 1.0 / (main + 2.0 * side * root)


def split(fields, *fifths):
    cuts = sorted({0, *(fields * n // 5 for n in fifths), fields})
    return tuple(zip(cuts[:-1], cuts[1:]))


def pick(position, values):
    chosen = jnp.float32(values[-1])
    for index in range(len(values) - 1):
        chosen = jnp.where(position == index, jnp.float32(values[index]), chosen)
    return chosen


def kernel(
    sizes,
    lag_hbm,
    harm_hbm,
    state_hbm,
    coef_hbm,
    out_ref,
    u,
    co,
    flux,
    sums,
    got_sums,
    ax_own,
    ax_got,
    sp_left,
    sp_right,
    got_left,
    got_right,
    waves,
    lag_ref,
    harm_ref,
    pitch_ready,
    span_ready,
    next_ready,
    local_sem,
    send_sem,
    recv_sem,
):
    npitch, naxial, nspan = sizes
    fields, cells, rows, _ = u.shape
    tiles = rows // 8
    parts, span_parts = split(fields, *AXIAL_CUTS), split(fields, *SPAN_CUTS)
    harm_max = co.shape[1]
    total = cells * npitch
    diffusion = float(total * total // 64)
    r, r_scale = line_root(1.0, 0.25)
    q, q_scale = line_root(1.0 + 2.0 * diffusion, -diffusion)
    pitch, axial, span = (lax.axis_index(name) for name in ("pitch", "axial", "span"))

    state_copies = [
        pltpu.make_async_copy(state_hbm.at[f], u.at[f], local_sem.at[0]) for f in range(fields)
    ]
    state_copy = pltpu.make_async_copy(state_hbm, u, local_sem.at[0])
    coef_copy = pltpu.make_async_copy(coef_hbm, co, local_sem.at[0])
    lag_copy = pltpu.make_async_copy(lag_hbm, lag_ref, local_sem.at[1])
    harm_copy = pltpu.make_async_copy(harm_hbm, harm_ref, local_sem.at[1])

    def when(flag, action):
        @pl.when(flag)
        def _():
            action()

    def both(*flags):
        return functools.reduce(jnp.logical_and, flags)

    def no(flag):
        return jnp.logical_not(flag)

    paired = npitch % 2 == 0 and naxial % 2 == 0
    has_up, has_down = axial > 0, axial < naxial - 1
    has_left, has_right = span > 0, span < nspan - 1
    odd = lax.rem(axial, 2) == 1
    even = no(odd)
    hub_block = both(even, axial + 2 < naxial)
    last_even = both(even, axial + 2 >= naxial)
    second = lax.rem(pitch, 2) == 1 if paired else pitch >= 0
    first = no(second)
    hub = both(hub_block, second)
    far_hub = both(odd, second, axial > 2)
    under_hub = both(odd, has_down)

    for copy in state_copies:
        copy.start()
    lag_copy.start()
    barrier = pltpu.get_barrier_semaphore()

    def tell(semaphore, **where):
        pl.semaphore_signal(semaphore, inc=1, device_id=where, device_id_type=MESH)

    def count(*flags):
        return sum(jnp.where(flag, 1, 0) for flag in flags)

    told_axial, told_pitch = jnp.where(odd, axial - 1, axial - 2), pitch
    if paired:
        told_axial = jnp.where(both(first, even), axial + 1, told_axial)
        told_axial = jnp.where(both(first, under_hub), axial + 2, told_axial)
        told_pitch = jnp.where(both(first, jnp.logical_or(even, has_down)), pitch + 1, pitch)
    when(has_up, lambda: tell(barrier, axial=told_axial, pitch=told_pitch))
    when(has_down, lambda: tell(barrier, axial=axial + 1))
    when(has_right, lambda: tell(barrier, span=span + 1))
    for other in range(npitch - 1):
        when(other < pitch, lambda: tell(barrier, pitch=jnp.int32(other)))

    heard = count(has_left, has_up, both(last_even, has_down))
    heard = heard + 2 * count(hub) + (npitch - 1 - pitch)
    if paired:
        heard = heard + 2 * count(far_hub)
    pl.semaphore_wait(barrier, heard)

    def remote(src, dst, sent, got, **where):
        return pltpu.make_async_remote_copy(
            src_ref=src,
            dst_ref=dst,
            send_sem=send_sem.at[sent],
            recv_sem=recv_sem.at[got],
            device_id=where,
            device_id_type=MESH,
        )

    def axial_part(src, from_row, to_row, sent, got, some, target):
        return remote(
            src.at[some, :, from_row : from_row + 4, :],
            ax_got.at[some, :, to_row : to_row + 4, :],
            sent,
            got,
            axial=target,
        )

    down_copies, up_copies, soon_copies = [], [], []
    for k, part in enumerate(parts):
        some = slice(*part)
        down_copies.append(axial_part(u, rows - 4, 0, 0, 2 * k, some, axial + 1))
        up_copies.append(axial_part(u, 0, 4, 1, 2 * k + 1, some, axial - 1))
        soon_copies.append(axial_part(state_hbm, 0, 4, 1, 2 * k + 1, some, axial - 1))
    down_sent = axial_part(u, rows - 4, 0, 0, 0, slice(0, fields), axial + 1)
    up_sent = axial_part(u, 0, 4, 1, 1, slice(0, fields), axial - 1)
    slots = 2 * len(parts)
    right_copy = remote(sp_right, got_left, 2, slots, span=span + 1)
    left_copies = []
    for k, part in enumerate(span_parts):
        some = slice(*part)
        left_copies.append(
            remote(sp_left.at[some], got_right.at[some], 3, slots + 1 + k, span=span - 1)
        )
    left_sent = remote(sp_left, got_right, 3, slots + 1, span=span - 1)
    slots = slots + 1 + len(span_parts)

    def start_all(copies):
        for copy in copies:
            copy.start()

    when(odd, lambda: start_all(soon_copies))
    if paired:
        when(far_hub, lambda: tell(next_ready, axial=axial - 2, pitch=pitch - 1))
    when(hub, lambda: tell(next_ready, axial=axial + 1))
    when(both(under_hub, first), lambda: tell(next_ready, axial=axial - 1))
    when(has_left, lambda: tell(span_ready, span=span - 1))
    for other in range(1, npitch):
        when(other > pitch, lambda: tell(pitch_ready, pitch=jnp.int32(other)))
    row = lax.broadcasted_iota(jnp.int32, (8, 128), 0)
    lane = lax.broadcasted_iota(jnp.int32, (8, 128), 1)
    group, place = lane // 4, lane % 4
    low_rows = row < 4

    state_copy.wait()
    when(both(even, has_up), lambda: start_all(up_copies))
    when(both(has_down, even, no(both(hub_block, first))), lambda: start_all(down_copies))

    groups = sp_left.shape[1]

    def pack_span(f, carry):
        for g in range(groups):
            right = left = jnp.zeros((8, 128), jnp.float32)
            for k in range(32):
                i, t = divmod(g * 32 + k, tiles)
                moved = pltpu.roll(u[f, i, t * 8 : t * 8 + 8, :], (4 * k + 4) % 128, 1)
                right = jnp.where(group == k, moved, right)
                left = jnp.where(group == (k + 1) % 32, moved, left)
            sp_right[f, g] = right
            sp_left[f, g] = left
        return carry

    for k, part in enumerate(span_parts):
        for f in range(*part):
            pack_span(f, 0)
        when(has_left, left_copies[k].start)
    coef_copy.start()
    lag_copy.wait()
    harm_copy.start()

    def flux_tile(t, carry):
        at = pl.ds(pl.multiple_of(t * 8, 8), 8)
        parts = [None] * 4
        for i in range(cells):
            cell = [u[f, i, at, :] for f in range(fields)]
            inverse = 1.0 / cell[0]
            speed = cell[2] * inverse
            kinetic = 0.5 * (cell[1] * cell[1] + cell[2] * cell[2] + cell[3] * cell[3]) * inverse
            pressure = (HEAT_RATIO_GAS - 1.0) * (cell[4] - kinetic)
            values = [
                cell[2],
                cell[1] * speed,
                cell[2] * speed + pressure,
                cell[3] * speed,
                (cell[4] + pressure) * speed,
            ]
            for f in range(fields):
                flux[f, i, at, :] = values[f]
            if i == 0:
                parts = [list(values), list(values), list(cell), list(cell)]
            else:
                for f in range(fields):
                    parts[0][f] = r * parts[0][f] + values[f]
                    parts[1][f] = parts[1][f] + (r**i) * values[f]
                    parts[2][f] = q * parts[2][f] + cell[f]
                    parts[3][f] = parts[3][f] + (q**i) * cell[f]
        for s in range(4):
            for f in range(fields):
                sums[s, f, at, :] = parts[s][f]
        return carry

    lax.fori_loop(0, tiles, flux_tile, 0, unroll=True)

    sum_copies = [
        remote(sums, got_sums.at[step - 1], 3 + step, slots - 1 + step, pitch=lax.rem(pitch + step, npitch))
        for step in range(1, npitch)
    ]
    when(pitch > 0, lambda: pl.semaphore_wait(pitch_ready, pitch))
    for copy in sum_copies:
        copy.start()

    def clear(ref):
        ref[...] = jnp.zeros_like(ref)

    when(no(has_up), lambda: clear(ax_got.at[:, :, :4, :]))
    when(no(has_down), lambda: clear(ax_got.at[:, :, 4:, :]))
    when(no(has_left), lambda: clear(got_left))
    when(no(has_right), lambda: clear(got_right))

    weight = -DAMPING / 256.0

    def damp_field(f, carry):
        for i in range(cells):
            x = u[f, i]
            result = (140.0 * weight) * x
            for o, c in ((1, -56.0), (2, 28.0), (3, -8.0), (4, 1.0)):
                pair = (pltpu.roll(x, o, 0) + pltpu.roll(x, rows - o, 0)) + (
                    pltpu.roll(x, o, 1) + pltpu.roll(x, 128 - o, 1)
                )
                result = result + (c * weight) * pair
            out_ref[f, i] = result
            ends = jnp.where(low_rows, x[:8, :], x[rows - 8 :, :])
            ax_own[f, i] = -pltpu.roll(ends, 4, 0)
        return carry

    @pl.when(jnp.logical_or(under_hub, both(hub_block, first)))
    def _():
        pl.semaphore_wait(next_ready, 1)
        start_all(down_copies)

    damp_field(0, 0)
    damp_field(1, 0)

    @pl.when(has_right)
    def _():
        pl.semaphore_wait(span_ready, 1)
        right_copy.start()

    for f in range(2, fields):
        damp_field(f, 0)

    harm_copy.wait()
    order = row.astype(jnp.float32) + 1.0
    phase = (2.0 * math.pi / PERIOD_SAMPLES) * order * lag_ref[0].astype(jnp.float32)
    active = row < harm_ref[...]
    waves[0] = jnp.where(active, jnp.cos(phase), 0.0)
    waves[1] = jnp.where(active, jnp.sin(phase), 0.0)
    near_first = pick(pitch, [r ** (cells * p) for p in range(npitch)])
    near_last = pick(pitch, [r ** (cells * (npitch - 1 - p)) for p in range(npitch)])
    jump_scale = -STEP_RATE * 0.75 * r_scale / (1.0 - r**total)
    jump_weights = [
        near_first * (jump_scale * (r**i + r ** (i + 1)))
        + near_last * (jump_scale * (r ** (cells - i) + r ** (cells - 1 - i)))
        for i in range(cells)
    ]
    flux_scale = -STEP_RATE * 0.75 * r_scale * (r - 1.0 / r)

    coef_copy.wait()

    def solve_field(f, carry):
        for t in range(tiles):
            at = pl.ds(t * 8, 8)
            jump = None
            for part in range(2):
                for k in range(harm_max):
                    term = waves[part, pl.ds(k, 1), :] * co[part, k, f, at, :]
                    jump = term if jump is None else jump + term
            x = [u[f, i, at, :] for i in range(cells)]
            y = [flux[f, i, at, :] for i in range(cells)]
            back_x, back_y = [None] * cells, [None] * cells
            carry_x, carry_y = q * x[cells - 1], y[cells - 1]
            for i in reversed(range(cells - 1)):
                back_x[i], back_y[i] = carry_x, carry_y
                if i > 0:
                    carry_x = q * (x[i] + carry_x)
                    carry_y = y[i] + r * carry_y
            front_x, front_y = None, None
            for i in range(cells):
                front_x = x[i] if front_x is None else x[i] + q * front_x
                value = out_ref[f, i, at, :] + jump_weights[i] * jump
                relaxed = front_x if back_x[i] is None else front_x + back_x[i]
                value = value + q_scale * relaxed
                slope = front_y
                if back_y[i] is not None:
                    slope = -back_y[i] if slope is None else slope - back_y[i]
                value = value + (flux_scale * r) * slope
                front_y = y[i] if front_y is None else y[i] + r * front_y
                out_ref[f, i, at, :] = value
        return carry

    lax.fori_loop(0, fields, solve_field, 0, unroll=True)

    for copy in sum_copies:
        copy.wait_recv()
    r_wrap = 1.0 / (1.0 - r**total)
    q_wrap = 1.0 / (1.0 - q**total)

    def carry_field(f, carry):
        for t in range(tiles):
            at = pl.ds(t * 8, 8)
            joined = []
            for s, (root, wrap) in enumerate(
                ((r, r_wrap), (r, r_wrap), (q, q_wrap), (q, q_wrap))
            ):
                value = (wrap * root ** (cells * (npitch - 1))) * sums[s, f, at, :]
                for step in range(1, npitch):
                    distance = step - 1 if s % 2 == 0 else npitch - 1 - step
                    factor = wrap * root ** (cells * distance)
                    value = value + factor * got_sums[step - 1, s, f, at, :]
                joined.append(value)
            for i in range(cells):
                out_ref[f, i, at, :] = (
                    out_ref[f, i, at, :]
                    + (flux_scale * r ** (i + 1)) * joined[0]
                    - (flux_scale * r ** (cells - i)) * joined[1]
                    + (q_scale * q ** (i + 1)) * joined[2]
                    + (q_scale * q ** (cells - i)) * joined[3]
                )
        return carry

    lax.fori_loop(0, fields, carry_field, 0, unroll=True)

    outer = jnp.logical_or(lane < 4, lane >= 124)
    from_left = [jnp.where(place + t < 4, EDGE[t] * weight, 0.0) for t in range(4)]
    from_right = [jnp.where(place >= t, EDGE[t] * weight, 0.0) for t in range(4)]
    even_group = group % 2 == 0

    def span_field(f, carry):
        for g in range(groups):
            before = got_left[f, g] - sp_right[f, g]
            after = got_right[f, g] - sp_left[f, g]
            starts, stops = from_left[0] * before, from_right[0] * after
            for t in range(1, 4):
                starts = starts + from_left[t] * pltpu.roll(before, 128 - t, 1)
                stops = stops + from_right[t] * pltpu.roll(after, t, 1)
            stops = pltpu.roll(stops, 120, 1)
            ends = (
                jnp.where(even_group, starts, stops),
                jnp.where(even_group, stops, starts),
            )
            for k in range(32):
                i, t = divmod(g * 32 + k, tiles)
                moved = pltpu.roll(ends[k % 2], (128 - 4 * k) % 128, 1)
                out_ref[f, i, t * 8 : t * 8 + 8, :] += jnp.where(outer, moved, 0.0)
        return carry

    def span_ends():
        when(has_left, right_copy.wait_recv)
        for k, part in enumerate(span_parts):
            when(has_right, left_copies[k].wait_recv)
            for f in range(*part):
                span_field(f, 0)

    corner = both(axial == 0, span == 0)
    when(no(corner), span_ends)

    near_low = [jnp.where(row + t < 4, EDGE[t] * weight, 0.0) for t in range(1, 4)]
    near_high = [jnp.where(row >= 4 + t, EDGE[t] * weight, 0.0) for t in range(1, 4)]

    def axial_field(f, carry):
        for i in range(cells):
            delta = ax_got[f, i] + ax_own[f, i]
            ends = (EDGE[0] * weight) * delta
            for t in range(1, 4):
                ends = ends + near_low[t - 1] * pltpu.roll(delta, 8 - t, 0)
                ends = ends + near_high[t - 1] * pltpu.roll(delta, t, 0)
            out_ref[f, i, :8, :] += jnp.where(low_rows, ends, 0.0)
            out_ref[f, i, rows - 8 :, :] += jnp.where(low_rows, 0.0, ends)
        return carry

    for k, part in enumerate(parts):
        when(has_up, down_copies[k].wait_recv)
        when(has_down, up_copies[k].wait_recv)
        for f in range(*part):
            axial_field(f, 0)
    when(corner, span_ends)

    for copy in sum_copies:
        copy.wait_send()
    when(has_down, down_sent.wait_send)
    when(has_up, up_sent.wait_send)
    when(has_right, right_copy.wait_send)
    when(has_left, left_sent.wait_send)


def shards(sizes, state, coeffs, lag_shift, harmonics):
    fields, cells, rows, lanes = state.shape
    npitch = sizes[0]
    groups = cells * (rows // 8) // 32
    vmem = lambda *shape: pltpu.VMEM(shape, jnp.float32)
    halo = (fields, cells, 8, lanes)
    packed = (fields, groups, 8, lanes)
    arrivals = 2 * len(split(fields, *AXIAL_CUTS)) + 1 + len(split(fields, *SPAN_CUTS)) + npitch - 1
    return pl.pallas_call(
        functools.partial(kernel, sizes),
        out_shape=pltpu.VMEM(state.shape, jnp.float32),
        in_specs=[
            pl.BlockSpec(memory_space=pltpu.HBM),
            pl.BlockSpec(memory_space=pltpu.HBM),
            pl.BlockSpec(memory_space=pltpu.HBM),
            pl.BlockSpec(memory_space=pltpu.HBM),
        ],
        out_specs=pl.BlockSpec(memory_space=pltpu.VMEM),
        scratch_shapes=[
            vmem(*state.shape),
            vmem(*coeffs.shape),
            vmem(*state.shape),
            vmem(4, fields, rows, lanes),
            vmem(npitch - 1, 4, fields, rows, lanes),
            vmem(*halo),
            vmem(*halo),
            vmem(*packed),
            vmem(*packed),
            vmem(*packed),
            vmem(*packed),
            vmem(2, 8, lanes),
            pltpu.SMEM((1,), jnp.int32),
            pltpu.VMEM((1, lanes), jnp.int32),
            pltpu.SemaphoreType.REGULAR,
            pltpu.SemaphoreType.REGULAR,
            pltpu.SemaphoreType.REGULAR,
            pltpu.SemaphoreType.DMA((2,)),
            pltpu.SemaphoreType.DMA((4 + npitch - 1,)),
            pltpu.SemaphoreType.DMA((arrivals,)),
        ],
        compiler_params=pltpu.CompilerParams(collective_id=0, has_side_effects=True),
    )(lag_shift, harmonics.reshape(1, lanes), state, coeffs)


def solution(mesh):
    sizes = tuple(mesh.shape[name] for name in ("pitch", "axial", "span"))
    placed = (
        P(None, "pitch", "axial", "span"),
        P(None, None, None, "axial", "span"),
        P(),
        P("span"),
    )
    return jax.shard_map(
        functools.partial(shards, sizes),
        mesh=mesh,
        in_specs=placed,
        out_specs=P(None, "pitch", "axial", "span"),
        check_vma=False,
    )
```

```python
import functools
import math

import jax
import jax.numpy as jnp
from jax import lax
from jax.experimental import pallas as pl
from jax.experimental.pallas import tpu as pltpu
from jax.sharding import PartitionSpec as P

PERIOD_SAMPLES = 64
HEAT_RATIO_GAS = 1.4
STEP_RATE = 0.25
DAMPING = 0.5
EDGE = (1.0, -8.0, 28.0, -56.0)
MESH = pl.DeviceIdType.MESH
AXIAL_CUTS, SPAN_CUTS = (4,), (3,)


def line_root(main, side):
    root = (-main + math.sqrt(main * main - 4.0 * side * side)) / (2.0 * side)
    return root, 1.0 / (main + 2.0 * side * root)


def split(fields, *fifths):
    cuts = sorted({0, *(fields * n // 5 for n in fifths), fields})
    return tuple(zip(cuts[:-1], cuts[1:]))


def pick(position, values):
    chosen = jnp.float32(values[-1])
    for index in range(len(values) - 1):
        chosen = jnp.where(position == index, jnp.float32(values[index]), chosen)
    return chosen


def kernel(
    sizes,
    lag_hbm,
    harm_hbm,
    state_hbm,
    coef_hbm,
    out_ref,
    u,
    co,
    flux,
    sums,
    got_sums,
    ax_own,
    ax_got,
    sp_left,
    sp_right,
    got_left,
    got_right,
    waves,
    lag_ref,
    harm_ref,
    pitch_ready,
    span_ready,
    next_ready,
    local_sem,
    send_sem,
    recv_sem,
):
    npitch, naxial, nspan = sizes
    fields, cells, rows, _ = u.shape
    tiles = rows // 8
    parts, span_parts = split(fields, *AXIAL_CUTS), split(fields, *SPAN_CUTS)
    harm_max = co.shape[1]
    total = cells * npitch
    diffusion = float(total * total // 64)
    r, r_scale = line_root(1.0, 0.25)
    q, q_scale = line_root(1.0 + 2.0 * diffusion, -diffusion)
    pitch, axial, span = (lax.axis_index(name) for name in ("pitch", "axial", "span"))

    state_copies, part_copies = [], []
    for k, part in enumerate(span_parts):
        some = slice(*part)
        part_copies.append(pltpu.make_async_copy(state_hbm.at[some], u.at[some], local_sem.at[k]))
        for f in range(*part):
            state_copies.append(
                pltpu.make_async_copy(state_hbm.at[f], u.at[f], local_sem.at[k])
            )
    coef_copy = pltpu.make_async_copy(coef_hbm, co, local_sem.at[0])
    lag_copy = pltpu.make_async_copy(lag_hbm, lag_ref, local_sem.at[1])
    harm_copy = pltpu.make_async_copy(harm_hbm, harm_ref, local_sem.at[1])

    def when(flag, action):
        @pl.when(flag)
        def _():
            action()

    def both(*flags):
        return functools.reduce(jnp.logical_and, flags)

    def no(flag):
        return jnp.logical_not(flag)

    paired = npitch % 2 == 0 and naxial % 2 == 0
    has_up, has_down = axial > 0, axial < naxial - 1
    has_left, has_right = span > 0, span < nspan - 1
    odd = lax.rem(axial, 2) == 1
    even = no(odd)
    hub_block = both(even, axial + 2 < naxial)
    last_even = both(even, axial + 2 >= naxial)
    second = lax.rem(pitch, 2) == 1 if paired else pitch >= 0
    first = no(second)
    hub = both(hub_block, second)
    far_hub = both(odd, second, axial > 2)
    under_hub = both(odd, has_down)

    for copy in state_copies:
        copy.start()
    barrier = pltpu.get_barrier_semaphore()

    def tell(semaphore, **where):
        pl.semaphore_signal(semaphore, inc=1, device_id=where, device_id_type=MESH)

    def count(*flags):
        return sum(jnp.where(flag, 1, 0) for flag in flags)

    told_axial, told_pitch = jnp.where(odd, axial - 1, axial - 2), pitch
    if paired:
        told_axial = jnp.where(both(first, even), axial + 1, told_axial)
        told_axial = jnp.where(both(first, under_hub), axial + 2, told_axial)
        told_pitch = jnp.where(both(first, jnp.logical_or(even, has_down)), pitch + 1, pitch)
    when(has_up, lambda: tell(barrier, axial=told_axial, pitch=told_pitch))
    when(has_down, lambda: tell(barrier, axial=axial + 1))
    when(has_right, lambda: tell(barrier, span=span + 1))
    for other in range(npitch - 1):
        when(other < pitch, lambda: tell(barrier, pitch=jnp.int32(other)))

    heard = count(has_left, has_up, both(last_even, has_down))
    heard = heard + 2 * count(hub) + (npitch - 1 - pitch)
    if paired:
        heard = heard + 2 * count(far_hub)
    pl.semaphore_wait(barrier, heard)

    def remote(src, dst, sent, got, **where):
        return pltpu.make_async_remote_copy(
            src_ref=src,
            dst_ref=dst,
            send_sem=send_sem.at[sent],
            recv_sem=recv_sem.at[got],
            device_id=where,
            device_id_type=MESH,
        )

    def axial_part(src, from_row, to_row, sent, got, some, target):
        return remote(
            src.at[some, :, from_row : from_row + 4, :],
            ax_got.at[some, :, to_row : to_row + 4, :],
            sent,
            got,
            axial=target,
        )

    down_copies, up_copies, soon_copies = [], [], []
    for k, part in enumerate(parts):
        some = slice(*part)
        down_copies.append(axial_part(u, rows - 4, 0, 0, 2 * k, some, axial + 1))
        up_copies.append(axial_part(u, 0, 4, 1, 2 * k + 1, some, axial - 1))
        soon_copies.append(axial_part(state_hbm, 0, 4, 1, 2 * k + 1, some, axial - 1))
    down_sent = axial_part(u, rows - 4, 0, 0, 0, slice(0, fields), axial + 1)
    up_sent = axial_part(u, 0, 4, 1, 1, slice(0, fields), axial - 1)
    slots = 2 * len(parts)
    right_copy = remote(sp_right, got_left, 2, slots, span=span + 1)
    left_copies = []
    for k, part in enumerate(span_parts):
        some = slice(*part)
        left_copies.append(
            remote(sp_left.at[some], got_right.at[some], 3, slots + 1 + k, span=span - 1)
        )
    left_sent = remote(sp_left, got_right, 3, slots + 1, span=span - 1)
    slots = slots + 1 + len(span_parts)

    def start_all(copies):
        for copy in copies:
            copy.start()

    held = both(under_hub, first, has_left)
    when(odd, lambda: start_all(soon_copies[:-1]))
    when(both(odd, no(held)), soon_copies[-1].start)
    if paired:
        when(far_hub, lambda: tell(next_ready, axial=axial - 2, pitch=pitch - 1))
    when(hub, lambda: tell(next_ready, axial=axial + 1))
    when(both(under_hub, first), lambda: tell(next_ready, axial=axial - 1))
    when(has_left, lambda: tell(span_ready, span=span - 1))
    for other in range(1, npitch):
        when(other > pitch, lambda: tell(pitch_ready, pitch=jnp.int32(other)))
    row = lax.broadcasted_iota(jnp.int32, (8, 128), 0)
    lane = lax.broadcasted_iota(jnp.int32, (8, 128), 1)
    group, place = lane // 4, lane % 4
    low_rows = row < 4

    late = both(even, no(both(hub_block, first)))

    @pl.when(late)
    def _():
        for copy in part_copies:
            copy.wait()
        when(has_up, lambda: start_all(up_copies))
        when(has_down, lambda: start_all(down_copies))

    groups = sp_left.shape[1]

    def pack_span(f, carry):
        for g in range(groups):
            right = left = jnp.zeros((8, 128), jnp.float32)
            for k in range(32):
                i, t = divmod(g * 32 + k, tiles)
                moved = pltpu.roll(u[f, i, t * 8 : t * 8 + 8, :], (4 * k + 4) % 128, 1)
                right = jnp.where(group == k, moved, right)
                left = jnp.where(group == (k + 1) % 32, moved, left)
            sp_right[f, g] = right
            sp_left[f, g] = left
        return carry

    for k, part in enumerate(span_parts):
        when(no(late), part_copies[k].wait)
        for f in range(*part):
            pack_span(f, 0)
        when(has_left, left_copies[k].start)
    when(both(even, has_up, no(late)), lambda: start_all(up_copies))
    coef_copy.start()
    lag_copy.start()

    ahead = both(under_hub, second, has_left)

    @pl.when(ahead)
    def _():
        pl.semaphore_wait(next_ready, 1)
        start_all(down_copies)

    def flux_tile(t, carry):
        at = pl.ds(pl.multiple_of(t * 8, 8), 8)
        parts = [None] * 4
        for i in range(cells):
            cell = [u[f, i, at, :] for f in range(fields)]
            inverse = 1.0 / cell[0]
            speed = cell[2] * inverse
            kinetic = 0.5 * (cell[1] * cell[1] + cell[2] * cell[2] + cell[3] * cell[3]) * inverse
            pressure = (HEAT_RATIO_GAS - 1.0) * (cell[4] - kinetic)
            values = [
                cell[2],
                cell[1] * speed,
                cell[2] * speed + pressure,
                cell[3] * speed,
                (cell[4] + pressure) * speed,
            ]
            for f in range(fields):
                flux[f, i, at, :] = values[f]
            if i == 0:
                parts = [list(values), list(values), list(cell), list(cell)]
            else:
                for f in range(fields):
                    parts[0][f] = r * parts[0][f] + values[f]
                    parts[1][f] = parts[1][f] + (r**i) * values[f]
                    parts[2][f] = q * parts[2][f] + cell[f]
                    parts[3][f] = parts[3][f] + (q**i) * cell[f]
        for s in range(4):
            for f in range(fields):
                sums[s, f, at, :] = parts[s][f]
        return carry

    lax.fori_loop(0, tiles, flux_tile, 0, unroll=True)

    sum_copies = [
        remote(sums, got_sums.at[step - 1], 3 + step, slots - 1 + step, pitch=lax.rem(pitch + step, npitch))
        for step in range(1, npitch)
    ]
    when(pitch > 0, lambda: pl.semaphore_wait(pitch_ready, pitch))
    for copy in sum_copies:
        copy.start()

    def clear(ref):
        ref[...] = jnp.zeros_like(ref)

    when(no(has_up), lambda: clear(ax_got.at[:, :, :4, :]))
    when(no(has_down), lambda: clear(ax_got.at[:, :, 4:, :]))
    when(no(has_left), lambda: clear(got_left))
    when(no(has_right), lambda: clear(got_right))

    weight = -DAMPING / 256.0

    def damp_field(f, carry):
        for i in range(cells):
            x = u[f, i]
            result = (140.0 * weight) * x
            for o, c in ((1, -56.0), (2, 28.0), (3, -8.0), (4, 1.0)):
                pair = (pltpu.roll(x, o, 0) + pltpu.roll(x, rows - o, 0)) + (
                    pltpu.roll(x, o, 1) + pltpu.roll(x, 128 - o, 1)
                )
                result = result + (c * weight) * pair
            out_ref[f, i] = result
            ends = jnp.where(low_rows, x[:8, :], x[rows - 8 :, :])
            ax_own[f, i] = -pltpu.roll(ends, 4, 0)
        return carry

    @pl.when(jnp.logical_or(both(under_hub, no(ahead)), both(hub_block, first)))
    def _():
        pl.semaphore_wait(next_ready, 1)
        start_all(down_copies)

    when(held, soon_copies[-1].start)
    lag_copy.wait()
    harm_copy.start()

    damp_field(0, 0)
    damp_field(1, 0)

    @pl.when(has_right)
    def _():
        pl.semaphore_wait(span_ready, 1)
        right_copy.start()

    for f in range(2, fields):
        damp_field(f, 0)

    harm_copy.wait()
    order = row.astype(jnp.float32) + 1.0
    phase = (2.0 * math.pi / PERIOD_SAMPLES) * order * lag_ref[0].astype(jnp.float32)
    active = row < harm_ref[...]
    waves[0] = jnp.where(active, jnp.cos(phase), 0.0)
    waves[1] = jnp.where(active, jnp.sin(phase), 0.0)
    near_first = pick(pitch, [r ** (cells * p) for p in range(npitch)])
    near_last = pick(pitch, [r ** (cells * (npitch - 1 - p)) for p in range(npitch)])
    jump_scale = -STEP_RATE * 0.75 * r_scale / (1.0 - r**total)
    jump_weights = [
        near_first * (jump_scale * (r**i + r ** (i + 1)))
        + near_last * (jump_scale * (r ** (cells - i) + r ** (cells - 1 - i)))
        for i in range(cells)
    ]
    flux_scale = -STEP_RATE * 0.75 * r_scale * (r - 1.0 / r)

    coef_copy.wait()

    def solve_field(f, carry):
        for t in range(tiles):
            at = pl.ds(t * 8, 8)
            jump = None
            for part in range(2):
                for k in range(harm_max):
                    term = waves[part, pl.ds(k, 1), :] * co[part, k, f, at, :]
                    jump = term if jump is None else jump + term
            x = [u[f, i, at, :] for i in range(cells)]
            y = [flux[f, i, at, :] for i in range(cells)]
            back_x, back_y = [None] * cells, [None] * cells
            carry_x, carry_y = q * x[cells - 1], y[cells - 1]
            for i in reversed(range(cells - 1)):
                back_x[i], back_y[i] = carry_x, carry_y
                if i > 0:
                    carry_x = q * (x[i] + carry_x)
                    carry_y = y[i] + r * carry_y
            front_x, front_y = None, None
            for i in range(cells):
                front_x = x[i] if front_x is None else x[i] + q * front_x
                value = out_ref[f, i, at, :] + jump_weights[i] * jump
                relaxed = front_x if back_x[i] is None else front_x + back_x[i]
                value = value + q_scale * relaxed
                slope = front_y
                if back_y[i] is not None:
                    slope = -back_y[i] if slope is None else slope - back_y[i]
                value = value + (flux_scale * r) * slope
                front_y = y[i] if front_y is None else y[i] + r * front_y
                out_ref[f, i, at, :] = value
        return carry

    lax.fori_loop(0, fields, solve_field, 0, unroll=True)

    for copy in sum_copies:
        copy.wait_recv()
    r_wrap = 1.0 / (1.0 - r**total)
    q_wrap = 1.0 / (1.0 - q**total)

    def carry_field(f, carry):
        for t in range(tiles):
            at = pl.ds(t * 8, 8)
            joined = []
            for s, (root, wrap) in enumerate(
                ((r, r_wrap), (r, r_wrap), (q, q_wrap), (q, q_wrap))
            ):
                value = (wrap * root ** (cells * (npitch - 1))) * sums[s, f, at, :]
                for step in range(1, npitch):
                    distance = step - 1 if s % 2 == 0 else npitch - 1 - step
                    factor = wrap * root ** (cells * distance)
                    value = value + factor * got_sums[step - 1, s, f, at, :]
                joined.append(value)
            for i in range(cells):
                out_ref[f, i, at, :] = (
                    out_ref[f, i, at, :]
                    + (flux_scale * r ** (i + 1)) * joined[0]
                    - (flux_scale * r ** (cells - i)) * joined[1]
                    + (q_scale * q ** (i + 1)) * joined[2]
                    + (q_scale * q ** (cells - i)) * joined[3]
                )
        return carry

    lax.fori_loop(0, fields, carry_field, 0, unroll=True)

    outer = jnp.logical_or(lane < 4, lane >= 124)
    from_left = [jnp.where(place + t < 4, EDGE[t] * weight, 0.0) for t in range(4)]
    from_right = [jnp.where(place >= t, EDGE[t] * weight, 0.0) for t in range(4)]
    even_group = group % 2 == 0

    def span_field(f, carry):
        for g in range(groups):
            before = got_left[f, g] - sp_right[f, g]
            after = got_right[f, g] - sp_left[f, g]
            starts, stops = from_left[0] * before, from_right[0] * after
            for t in range(1, 4):
                starts = starts + from_left[t] * pltpu.roll(before, 128 - t, 1)
                stops = stops + from_right[t] * pltpu.roll(after, t, 1)
            stops = pltpu.roll(stops, 120, 1)
            ends = (
                jnp.where(even_group, starts, stops),
                jnp.where(even_group, stops, starts),
            )
            for k in range(32):
                i, t = divmod(g * 32 + k, tiles)
                moved = pltpu.roll(ends[k % 2], (128 - 4 * k) % 128, 1)
                out_ref[f, i, t * 8 : t * 8 + 8, :] += jnp.where(outer, moved, 0.0)
        return carry

    def span_ends():
        when(has_left, right_copy.wait_recv)
        for k, part in enumerate(span_parts):
            when(has_right, left_copies[k].wait_recv)
            for f in range(*part):
                span_field(f, 0)

    corner = both(axial == 0, span == 0)
    when(no(corner), span_ends)

    near_low = [jnp.where(row + t < 4, EDGE[t] * weight, 0.0) for t in range(1, 4)]
    near_high = [jnp.where(row >= 4 + t, EDGE[t] * weight, 0.0) for t in range(1, 4)]

    def axial_field(f, carry):
        for i in range(cells):
            delta = ax_got[f, i] + ax_own[f, i]
            ends = (EDGE[0] * weight) * delta
            for t in range(1, 4):
                ends = ends + near_low[t - 1] * pltpu.roll(delta, 8 - t, 0)
                ends = ends + near_high[t - 1] * pltpu.roll(delta, t, 0)
            out_ref[f, i, :8, :] += jnp.where(low_rows, ends, 0.0)
            out_ref[f, i, rows - 8 :, :] += jnp.where(low_rows, 0.0, ends)
        return carry

    for k, part in enumerate(parts):
        when(has_up, down_copies[k].wait_recv)
        when(has_down, up_copies[k].wait_recv)
        for f in range(*part):
            axial_field(f, 0)
        if k == 0:
            when(corner, span_ends)

    for copy in sum_copies:
        copy.wait_send()
    when(has_down, down_sent.wait_send)
    when(has_up, up_sent.wait_send)
    when(has_right, right_copy.wait_send)
    when(has_left, left_sent.wait_send)


def shards(sizes, state, coeffs, lag_shift, harmonics):
    fields, cells, rows, lanes = state.shape
    npitch = sizes[0]
    groups = cells * (rows // 8) // 32
    vmem = lambda *shape: pltpu.VMEM(shape, jnp.float32)
    halo = (fields, cells, 8, lanes)
    packed = (fields, groups, 8, lanes)
    arrivals = 2 * len(split(fields, *AXIAL_CUTS)) + 1 + len(split(fields, *SPAN_CUTS)) + npitch - 1
    return pl.pallas_call(
        functools.partial(kernel, sizes),
        out_shape=pltpu.VMEM(state.shape, jnp.float32),
        in_specs=[
            pl.BlockSpec(memory_space=pltpu.HBM),
            pl.BlockSpec(memory_space=pltpu.HBM),
            pl.BlockSpec(memory_space=pltpu.HBM),
            pl.BlockSpec(memory_space=pltpu.HBM),
        ],
        out_specs=pl.BlockSpec(memory_space=pltpu.VMEM),
        scratch_shapes=[
            vmem(*state.shape),
            vmem(*coeffs.shape),
            vmem(*state.shape),
            vmem(4, fields, rows, lanes),
            vmem(npitch - 1, 4, fields, rows, lanes),
            vmem(*halo),
            vmem(*halo),
            vmem(*packed),
            vmem(*packed),
            vmem(*packed),
            vmem(*packed),
            vmem(2, 8, lanes),
            pltpu.SMEM((1,), jnp.int32),
            pltpu.VMEM((1, lanes), jnp.int32),
            pltpu.SemaphoreType.REGULAR,
            pltpu.SemaphoreType.REGULAR,
            pltpu.SemaphoreType.REGULAR,
            pltpu.SemaphoreType.DMA((2,)),
            pltpu.SemaphoreType.DMA((4 + npitch - 1,)),
            pltpu.SemaphoreType.DMA((arrivals,)),
        ],
        compiler_params=pltpu.CompilerParams(collective_id=0, has_side_effects=True),
    )(lag_shift, harmonics.reshape(1, lanes), state, coeffs)


def solution(mesh):
    sizes = tuple(mesh.shape[name] for name in ("pitch", "axial", "span"))
    placed = (
        P(None, "pitch", "axial", "span"),
        P(None, None, None, "axial", "span"),
        P(),
        P("span"),
    )
    return jax.shard_map(
        functools.partial(shards, sizes),
        mesh=mesh,
        in_specs=placed,
        out_specs=P(None, "pitch", "axial", "span"),
        check_vma=False,
    )
```

```python
import functools
import math

import jax
import jax.numpy as jnp
from jax import lax
from jax.experimental import pallas as pl
from jax.experimental.pallas import tpu as pltpu
from jax.sharding import PartitionSpec as P

PERIOD_SAMPLES = 64
HEAT_RATIO_GAS = 1.4
STEP_RATE = 0.25
DAMPING = 0.5
EDGE = (1.0, -8.0, 28.0, -56.0)
MESH = pl.DeviceIdType.MESH
AXIAL_CUTS, SPAN_CUTS = (3,), (2,)


def line_root(main, side):
    root = (-main + math.sqrt(main * main - 4.0 * side * side)) / (2.0 * side)
    return root, 1.0 / (main + 2.0 * side * root)


def split(fields, *fifths):
    cuts = sorted({0, *(fields * n // 5 for n in fifths), fields})
    return tuple(zip(cuts[:-1], cuts[1:]))


def pick(position, values):
    chosen = jnp.float32(values[-1])
    for index in range(len(values) - 1):
        chosen = jnp.where(position == index, jnp.float32(values[index]), chosen)
    return chosen


def kernel(
    sizes,
    lag_hbm,
    harm_hbm,
    state_hbm,
    coef_hbm,
    out_ref,
    u,
    co,
    flux,
    sums,
    got_sums,
    ax_own,
    ax_got,
    sp_left,
    sp_right,
    got_sides,
    waves,
    lag_ref,
    harm_ref,
    side_ready,
    next_ready,
    local_sem,
    send_sem,
    recv_sem,
):
    npitch, naxial, nspan = sizes
    fields, cells, rows, _ = u.shape
    tiles = rows // 8
    parts, span_parts = split(fields, *AXIAL_CUTS), split(fields, *SPAN_CUTS)
    harm_max = co.shape[1]
    total = cells * npitch
    diffusion = float(total * total // 64)
    r, r_scale = line_root(1.0, 0.25)
    q, q_scale = line_root(1.0 + 2.0 * diffusion, -diffusion)
    pitch, axial, span = (lax.axis_index(name) for name in ("pitch", "axial", "span"))

    pair = 2 if cells % 2 == 0 else 1
    state_copies, part_copies = [], []
    for k, part in enumerate(span_parts):
        some = slice(*part)
        part_copies.append(pltpu.make_async_copy(state_hbm.at[some], u.at[some], local_sem.at[k]))
        for f in range(*part):
            for i in range(0, cells, pair):
                some = (f, slice(i, i + pair))
                state_copies.append(
                    pltpu.make_async_copy(state_hbm.at[some], u.at[some], local_sem.at[k])
                )
    coef_copy = pltpu.make_async_copy(coef_hbm, co, local_sem.at[0])
    lag_copy = pltpu.make_async_copy(lag_hbm, lag_ref, local_sem.at[1])
    harm_copy = pltpu.make_async_copy(harm_hbm, harm_ref, local_sem.at[1])

    def when(flag, action):
        @pl.when(flag)
        def _():
            action()

    def both(*flags):
        return functools.reduce(jnp.logical_and, flags)

    def no(flag):
        return jnp.logical_not(flag)

    paired = npitch % 2 == 0 and naxial % 2 == 0
    has_up, has_down = axial > 0, axial < naxial - 1
    has_left, has_right = span > 0, span < nspan - 1
    odd = lax.rem(axial, 2) == 1
    even = no(odd)
    hub_block = both(even, axial + 2 < naxial)
    last_even = both(even, axial + 2 >= naxial)
    second = lax.rem(pitch, 2) == 1 if paired else pitch >= 0
    first = no(second)
    hub = both(hub_block, second)
    far_hub = both(odd, second, axial > 2)
    under_hub = both(odd, has_down)

    barrier = pltpu.get_barrier_semaphore()

    def tell(semaphore, **where):
        pl.semaphore_signal(semaphore, inc=1, device_id=where, device_id_type=MESH)

    def count(*flags):
        return sum(jnp.where(flag, 1, 0) for flag in flags)

    told_axial, told_pitch = jnp.where(odd, axial - 1, axial - 2), pitch
    if paired:
        told_axial = jnp.where(both(first, even), axial + 1, told_axial)
        told_axial = jnp.where(both(first, under_hub), axial + 2, told_axial)
        told_pitch = jnp.where(both(first, jnp.logical_or(even, has_down)), pitch + 1, pitch)
    when(has_up, lambda: tell(barrier, axial=told_axial, pitch=told_pitch))
    when(has_down, lambda: tell(barrier, axial=axial + 1))
    for copy in state_copies:
        copy.start()
    when(has_right, lambda: tell(barrier, span=span + 1))
    for other in range(npitch - 1):
        when(other < pitch, lambda: tell(barrier, pitch=jnp.int32(other)))

    heard = count(has_left, has_up, both(last_even, has_down))
    heard = heard + 2 * count(hub) + (npitch - 1 - pitch)
    if paired:
        heard = heard + 2 * count(far_hub)
    pl.semaphore_wait(barrier, heard)

    def remote(src, dst, sent, got, **where):
        return pltpu.make_async_remote_copy(
            src_ref=src,
            dst_ref=dst,
            send_sem=send_sem.at[sent],
            recv_sem=recv_sem.at[got],
            device_id=where,
            device_id_type=MESH,
        )

    def axial_part(src, from_row, to_row, sent, got, some, target):
        return remote(
            src.at[some, :, from_row : from_row + 4, :],
            ax_got.at[some, :, to_row : to_row + 4, :],
            sent,
            got,
            axial=target,
        )

    down_copies, up_copies, soon_copies = [], [], []
    for k, part in enumerate(parts):
        some = slice(*part)
        down_copies.append(axial_part(u, rows - 4, 0, 0, k, some, axial + 1))
        up_copies.append(axial_part(u, 0, 4, 0, k, some, axial - 1))
        soon_copies.append(axial_part(state_hbm, 0, 4, 0, k, some, axial - 1))

    def wait_axial(some, k, wait):
        for ways, flag in ((1, jnp.not_equal(has_up, has_down)), (2, both(has_up, has_down))):
            whole = ax_got.at[some, :, : 4 * ways, :]
            when(flag, lambda: wait(remote(whole, whole, 0, k, axial=axial)))

    slots = len(parts)
    got_left, got_right = got_sides.at[0], got_sides.at[1]
    right_copy = remote(sp_right, got_left, 1, slots, span=span + 1)
    left_copies = []
    for k, part in enumerate(span_parts):
        some = slice(*part)
        left_copies.append(
            remote(sp_left.at[some], got_right.at[some], 1, slots + 1 + k, span=span - 1)
        )

    def wait_span_sent():
        for ways, flag in (
            (1, jnp.not_equal(has_left, has_right)),
            (2, both(has_left, has_right)),
        ):
            whole = got_sides.at[:ways]
            when(flag, lambda: remote(whole, whole, 1, slots, span=span).wait_send())

    slots = slots + 1 + len(span_parts)

    def start_all(copies):
        for copy in copies:
            copy.start()

    held = both(under_hub, first, has_left)
    when(odd, lambda: start_all(soon_copies[:-1]))
    when(both(odd, no(held)), soon_copies[-1].start)
    if paired:
        when(far_hub, lambda: tell(next_ready, axial=axial - 2, pitch=pitch - 1))
    when(hub, lambda: tell(next_ready, axial=axial + 1))
    when(both(under_hub, first), lambda: tell(next_ready, axial=axial - 1))
    when(has_left, lambda: tell(side_ready, span=span - 1))
    for other in range(1, npitch):
        when(other > pitch, lambda: tell(side_ready, pitch=jnp.int32(other)))
    row = lax.broadcasted_iota(jnp.int32, (8, 128), 0)
    lane = lax.broadcasted_iota(jnp.int32, (8, 128), 1)
    group, place = lane // 4, lane % 4
    low_rows = row < 4

    late = both(even, no(both(hub_block, first)))

    @pl.when(late)
    def _():
        for copy in part_copies:
            copy.wait()
        when(has_up, lambda: start_all(up_copies))
        when(has_down, lambda: start_all(down_copies))

    groups = sp_left.shape[1]

    def pack_span(f, carry):
        for g in range(groups):
            right = left = jnp.zeros((8, 128), jnp.float32)
            for k in range(32):
                i, t = divmod(g * 32 + k, tiles)
                moved = pltpu.roll(u[f, i, t * 8 : t * 8 + 8, :], (4 * k + 4) % 128, 1)
                right = jnp.where(group == k, moved, right)
                left = jnp.where(group == (k + 1) % 32, moved, left)
            sp_right[f, g] = right
            sp_left[f, g] = left
        return carry

    for k, part in enumerate(span_parts):
        when(no(late), part_copies[k].wait)
        for f in range(*part):
            pack_span(f, 0)
        when(has_left, left_copies[k].start)
    when(both(even, has_up, no(late)), lambda: start_all(up_copies))
    coef_copy.start()
    lag_copy.start()

    ahead = both(under_hub, second, has_left)

    @pl.when(ahead)
    def _():
        pl.semaphore_wait(next_ready, 1)
        start_all(down_copies)

    def flux_tile(t, carry):
        at = pl.ds(pl.multiple_of(t * 8, 8), 8)
        parts = [None] * 4
        for i in range(cells):
            cell = [u[f, i, at, :] for f in range(fields)]
            inverse = 1.0 / cell[0]
            speed = cell[2] * inverse
            kinetic = 0.5 * (cell[1] * cell[1] + cell[2] * cell[2] + cell[3] * cell[3]) * inverse
            pressure = (HEAT_RATIO_GAS - 1.0) * (cell[4] - kinetic)
            values = [
                cell[2],
                cell[1] * speed,
                cell[2] * speed + pressure,
                cell[3] * speed,
                (cell[4] + pressure) * speed,
            ]
            for f in range(fields):
                flux[f, i, at, :] = values[f]
            if i == 0:
                parts = [list(values), list(values), list(cell), list(cell)]
            else:
                for f in range(fields):
                    parts[0][f] = r * parts[0][f] + values[f]
                    parts[1][f] = parts[1][f] + (r**i) * values[f]
                    parts[2][f] = q * parts[2][f] + cell[f]
                    parts[3][f] = parts[3][f] + (q**i) * cell[f]
        for s in range(4):
            for f in range(fields):
                sums[s, f, at, :] = parts[s][f]
        return carry

    lax.fori_loop(0, tiles, flux_tile, 0, unroll=True)

    sum_copies = [
        remote(sums, got_sums.at[step - 1], 1 + step, slots - 1 + step, pitch=lax.rem(pitch + step, npitch))
        for step in range(1, npitch)
    ]
    when(pitch == 0, lambda: start_all(sum_copies))

    def clear(ref):
        ref[...] = jnp.zeros_like(ref)

    when(no(has_up), lambda: clear(ax_got.at[:, :, :4, :]))
    when(no(has_down), lambda: clear(ax_got.at[:, :, 4:, :]))
    when(no(has_left), lambda: clear(got_left))
    when(no(has_right), lambda: clear(got_right))

    weight = -DAMPING / 256.0

    def damp_field(f, carry):
        for i in range(cells):
            x = u[f, i]
            result = (140.0 * weight) * x
            for o, c in ((1, -56.0), (2, 28.0), (3, -8.0), (4, 1.0)):
                pair = (pltpu.roll(x, o, 0) + pltpu.roll(x, rows - o, 0)) + (
                    pltpu.roll(x, o, 1) + pltpu.roll(x, 128 - o, 1)
                )
                result = result + (c * weight) * pair
            out_ref[f, i] = result
            ends = jnp.where(low_rows, x[:8, :], x[rows - 8 :, :])
            ax_own[f, i] = -pltpu.roll(ends, 4, 0)
        return carry

    @pl.when(jnp.logical_or(both(under_hub, no(ahead)), both(hub_block, first)))
    def _():
        pl.semaphore_wait(next_ready, 1)
        start_all(down_copies)

    when(held, soon_copies[-1].start)
    lag_copy.wait()
    harm_copy.start()

    damp_field(0, 0)
    damp_field(1, 0)

    sides = pitch + count(has_right)
    when(sides > 0, lambda: pl.semaphore_wait(side_ready, sides))
    when(pitch > 0, lambda: start_all(sum_copies))
    when(has_right, right_copy.start)

    for f in range(2, fields):
        damp_field(f, 0)

    harm_copy.wait()
    order = row.astype(jnp.float32) + 1.0
    phase = (2.0 * math.pi / PERIOD_SAMPLES) * order * lag_ref[0].astype(jnp.float32)
    active = row < harm_ref[...]
    waves[0] = jnp.where(active, jnp.cos(phase), 0.0)
    waves[1] = jnp.where(active, jnp.sin(phase), 0.0)
    near_first = pick(pitch, [r ** (cells * p) for p in range(npitch)])
    near_last = pick(pitch, [r ** (cells * (npitch - 1 - p)) for p in range(npitch)])
    jump_scale = -STEP_RATE * 0.75 * r_scale / (1.0 - r**total)
    jump_weights = [
        near_first * (jump_scale * (r**i + r ** (i + 1)))
        + near_last * (jump_scale * (r ** (cells - i) + r ** (cells - 1 - i)))
        for i in range(cells)
    ]
    flux_scale = -STEP_RATE * 0.75 * r_scale * (r - 1.0 / r)

    coef_copy.wait()

    def solve_field(f, carry):
        for t in range(tiles):
            at = pl.ds(t * 8, 8)
            jump = None
            for part in range(2):
                for k in range(harm_max):
                    term = waves[part, pl.ds(k, 1), :] * co[part, k, f, at, :]
                    jump = term if jump is None else jump + term
            x = [u[f, i, at, :] for i in range(cells)]
            y = [flux[f, i, at, :] for i in range(cells)]
            back_x, back_y = [None] * cells, [None] * cells
            carry_x, carry_y = q * x[cells - 1], y[cells - 1]
            for i in reversed(range(cells - 1)):
                back_x[i], back_y[i] = carry_x, carry_y
                if i > 0:
                    carry_x = q * (x[i] + carry_x)
                    carry_y = y[i] + r * carry_y
            front_x, front_y = None, None
            for i in range(cells):
                front_x = x[i] if front_x is None else x[i] + q * front_x
                value = out_ref[f, i, at, :] + jump_weights[i] * jump
                relaxed = front_x if back_x[i] is None else front_x + back_x[i]
                value = value + q_scale * relaxed
                slope = front_y
                if back_y[i] is not None:
                    slope = -back_y[i] if slope is None else slope - back_y[i]
                value = value + (flux_scale * r) * slope
                front_y = y[i] if front_y is None else y[i] + r * front_y
                out_ref[f, i, at, :] = value
        return carry

    lax.fori_loop(0, fields, solve_field, 0, unroll=True)

    for copy in sum_copies:
        copy.wait_recv()
    r_wrap = 1.0 / (1.0 - r**total)
    q_wrap = 1.0 / (1.0 - q**total)

    def carry_field(f, carry):
        for t in range(tiles):
            at = pl.ds(t * 8, 8)
            joined = []
            for s, (root, wrap) in enumerate(
                ((r, r_wrap), (r, r_wrap), (q, q_wrap), (q, q_wrap))
            ):
                value = (wrap * root ** (cells * (npitch - 1))) * sums[s, f, at, :]
                for step in range(1, npitch):
                    distance = step - 1 if s % 2 == 0 else npitch - 1 - step
                    factor = wrap * root ** (cells * distance)
                    value = value + factor * got_sums[step - 1, s, f, at, :]
                joined.append(value)
            for i in range(cells):
                out_ref[f, i, at, :] = (
                    out_ref[f, i, at, :]
                    + (flux_scale * r ** (i + 1)) * joined[0]
                    - (flux_scale * r ** (cells - i)) * joined[1]
                    + (q_scale * q ** (i + 1)) * joined[2]
                    + (q_scale * q ** (cells - i)) * joined[3]
                )
        return carry

    lax.fori_loop(0, fields, carry_field, 0, unroll=True)

    outer = jnp.logical_or(lane < 4, lane >= 124)
    from_left = [jnp.where(place + t < 4, EDGE[t] * weight, 0.0) for t in range(4)]
    from_right = [jnp.where(place >= t, EDGE[t] * weight, 0.0) for t in range(4)]
    even_group = group % 2 == 0

    def span_field(f, carry):
        for g in range(groups):
            before = got_left[f, g] - sp_right[f, g]
            after = got_right[f, g] - sp_left[f, g]
            starts, stops = from_left[0] * before, from_right[0] * after
            for t in range(1, 4):
                starts = starts + from_left[t] * pltpu.roll(before, 128 - t, 1)
                stops = stops + from_right[t] * pltpu.roll(after, t, 1)
            stops = pltpu.roll(stops, 120, 1)
            ends = (
                jnp.where(even_group, starts, stops),
                jnp.where(even_group, stops, starts),
            )
            for k in range(32):
                i, t = divmod(g * 32 + k, tiles)
                moved = pltpu.roll(ends[k % 2], (128 - 4 * k) % 128, 1)
                out_ref[f, i, t * 8 : t * 8 + 8, :] += jnp.where(outer, moved, 0.0)
        return carry

    def span_ends():
        when(has_left, right_copy.wait_recv)
        for k, part in enumerate(span_parts):
            when(has_right, left_copies[k].wait_recv)
            for f in range(*part):
                span_field(f, 0)

    span_ends()

    near_low = [jnp.where(row + t < 4, EDGE[t] * weight, 0.0) for t in range(1, 4)]
    near_high = [jnp.where(row >= 4 + t, EDGE[t] * weight, 0.0) for t in range(1, 4)]

    def axial_field(f, carry):
        for i in range(cells):
            delta = ax_got[f, i] + ax_own[f, i]
            ends = (EDGE[0] * weight) * delta
            for t in range(1, 4):
                ends = ends + near_low[t - 1] * pltpu.roll(delta, 8 - t, 0)
                ends = ends + near_high[t - 1] * pltpu.roll(delta, t, 0)
            out_ref[f, i, :8, :] += jnp.where(low_rows, ends, 0.0)
            out_ref[f, i, rows - 8 :, :] += jnp.where(low_rows, 0.0, ends)
        return carry

    for k, part in enumerate(parts):
        wait_axial(slice(*part), k, lambda copy: copy.wait_recv())
        for f in range(*part):
            axial_field(f, 0)

    for copy in sum_copies:
        copy.wait_send()
    wait_axial(slice(0, fields), 0, lambda copy: copy.wait_send())
    wait_span_sent()


def shards(sizes, state, coeffs, lag_shift, harmonics):
    fields, cells, rows, lanes = state.shape
    npitch = sizes[0]
    groups = cells * (rows // 8) // 32
    vmem = lambda *shape: pltpu.VMEM(shape, jnp.float32)
    halo = (fields, cells, 8, lanes)
    packed = (fields, groups, 8, lanes)
    arrivals = len(split(fields, *AXIAL_CUTS)) + 1 + len(split(fields, *SPAN_CUTS)) + npitch - 1
    return pl.pallas_call(
        functools.partial(kernel, sizes),
        out_shape=pltpu.VMEM(state.shape, jnp.float32),
        in_specs=[
            pl.BlockSpec(memory_space=pltpu.HBM),
            pl.BlockSpec(memory_space=pltpu.HBM),
            pl.BlockSpec(memory_space=pltpu.HBM),
            pl.BlockSpec(memory_space=pltpu.HBM),
        ],
        out_specs=pl.BlockSpec(memory_space=pltpu.VMEM),
        scratch_shapes=[
            vmem(*state.shape),
            vmem(*coeffs.shape),
            vmem(*state.shape),
            vmem(4, fields, rows, lanes),
            vmem(npitch - 1, 4, fields, rows, lanes),
            vmem(*halo),
            vmem(*halo),
            vmem(*packed),
            vmem(*packed),
            vmem(2, *packed),
            vmem(2, 8, lanes),
            pltpu.SMEM((1,), jnp.int32),
            pltpu.VMEM((1, lanes), jnp.int32),
            pltpu.SemaphoreType.REGULAR,
            pltpu.SemaphoreType.REGULAR,
            pltpu.SemaphoreType.DMA((2,)),
            pltpu.SemaphoreType.DMA((2 + npitch - 1,)),
            pltpu.SemaphoreType.DMA((arrivals,)),
        ],
        compiler_params=pltpu.CompilerParams(collective_id=0, has_side_effects=True),
    )(lag_shift, harmonics.reshape(1, lanes), state, coeffs)


def solution(mesh):
    sizes = tuple(mesh.shape[name] for name in ("pitch", "axial", "span"))
    placed = (
        P(None, "pitch", "axial", "span"),
        P(None, None, None, "axial", "span"),
        P(),
        P("span"),
    )
    return jax.shard_map(
        functools.partial(shards, sizes),
        mesh=mesh,
        in_specs=placed,
        out_specs=P(None, "pitch", "axial", "span"),
        check_vma=False,
    )
```

```python
import functools
import math

import jax
import jax.numpy as jnp
from jax import lax
from jax.experimental import pallas as pl
from jax.experimental.pallas import tpu as pltpu
from jax.sharding import PartitionSpec as P

PERIOD_SAMPLES = 64
HEAT_RATIO_GAS = 1.4
STEP_RATE = 0.25
DAMPING = 0.5
EDGE = (1.0, -8.0, 28.0, -56.0)
MESH = pl.DeviceIdType.MESH
AXIAL_CUTS, SPAN_CUTS = (4,), (2,)


def line_root(main, side):
    root = (-main + math.sqrt(main * main - 4.0 * side * side)) / (2.0 * side)
    return root, 1.0 / (main + 2.0 * side * root)


def split(fields, *fifths):
    cuts = sorted({0, *(fields * n // 5 for n in fifths), fields})
    return tuple(zip(cuts[:-1], cuts[1:]))


def pick(position, values):
    chosen = jnp.float32(values[-1])
    for index in range(len(values) - 1):
        chosen = jnp.where(position == index, jnp.float32(values[index]), chosen)
    return chosen


def kernel(
    sizes,
    lag_hbm,
    harm_hbm,
    state_hbm,
    coef_hbm,
    out_ref,
    u,
    co,
    flux,
    sums,
    got_sums,
    ax_own,
    ax_got,
    sp_left,
    sp_right,
    got_sides,
    waves,
    lag_ref,
    harm_ref,
    side_ready,
    next_ready,
    local_sem,
    send_sem,
    recv_sem,
):
    npitch, naxial, nspan = sizes
    fields, cells, rows, _ = u.shape
    tiles = rows // 8
    parts, span_parts = split(fields, *AXIAL_CUTS), split(fields, *SPAN_CUTS)
    harm_max = co.shape[1]
    total = cells * npitch
    diffusion = float(total * total // 64)
    r, r_scale = line_root(1.0, 0.25)
    q, q_scale = line_root(1.0 + 2.0 * diffusion, -diffusion)
    pitch, axial, span = (lax.axis_index(name) for name in ("pitch", "axial", "span"))

    pair = 2 if cells % 2 == 0 else 1
    state_copies, part_copies = [], []
    for k, part in enumerate(span_parts):
        some = slice(*part)
        part_copies.append(pltpu.make_async_copy(state_hbm.at[some], u.at[some], local_sem.at[k]))
        for f in range(*part):
            for i in range(0, cells, pair):
                some = (f, slice(i, i + pair))
                state_copies.append(
                    pltpu.make_async_copy(state_hbm.at[some], u.at[some], local_sem.at[k])
                )
    coef_copy = pltpu.make_async_copy(coef_hbm, co, local_sem.at[0])
    lag_copy = pltpu.make_async_copy(lag_hbm, lag_ref, local_sem.at[1])
    harm_copy = pltpu.make_async_copy(harm_hbm, harm_ref, local_sem.at[1])

    def when(flag, action):
        @pl.when(flag)
        def _():
            action()

    def both(*flags):
        return functools.reduce(jnp.logical_and, flags)

    def no(flag):
        return jnp.logical_not(flag)

    paired = npitch % 2 == 0 and naxial % 2 == 0
    has_up, has_down = axial > 0, axial < naxial - 1
    has_left, has_right = span > 0, span < nspan - 1
    odd = lax.rem(axial, 2) == 1
    even = no(odd)
    hub_block = both(even, axial + 2 < naxial)
    last_even = both(even, axial + 2 >= naxial)
    second = lax.rem(pitch, 2) == 1 if paired else pitch >= 0
    first = no(second)
    hub = both(hub_block, second)
    far_hub = both(odd, second, axial > 2)
    under_hub = both(odd, has_down)

    barrier = pltpu.get_barrier_semaphore()

    def tell(semaphore, **where):
        pl.semaphore_signal(semaphore, inc=1, device_id=where, device_id_type=MESH)

    def count(*flags):
        return sum(jnp.where(flag, 1, 0) for flag in flags)

    told_axial, told_pitch = jnp.where(odd, axial - 1, axial - 2), pitch
    if paired:
        told_axial = jnp.where(both(first, even), axial + 1, told_axial)
        told_axial = jnp.where(both(first, under_hub), axial + 2, told_axial)
        told_pitch = jnp.where(both(first, jnp.logical_or(even, has_down)), pitch + 1, pitch)
    when(has_up, lambda: tell(barrier, axial=told_axial, pitch=told_pitch))
    when(has_down, lambda: tell(barrier, axial=axial + 1))
    for copy in state_copies:
        copy.start()
    when(has_right, lambda: tell(barrier, span=span + 1))
    for other in range(npitch - 1):
        when(other < pitch, lambda: tell(barrier, pitch=jnp.int32(other)))

    heard = count(has_left, has_up, both(last_even, has_down))
    heard = heard + 2 * count(hub) + (npitch - 1 - pitch)
    if paired:
        heard = heard + 2 * count(far_hub)
    pl.semaphore_wait(barrier, heard)

    def remote(src, dst, sent, got, **where):
        return pltpu.make_async_remote_copy(
            src_ref=src,
            dst_ref=dst,
            send_sem=send_sem.at[sent],
            recv_sem=recv_sem.at[got],
            device_id=where,
            device_id_type=MESH,
        )

    def axial_part(src, from_row, to_row, sent, got, some, target):
        return remote(
            src.at[some, :, from_row : from_row + 4, :],
            ax_got.at[some, :, to_row : to_row + 4, :],
            sent,
            got,
            axial=target,
        )

    down_copies, up_copies, soon_copies = [], [], []
    for k, part in enumerate(parts):
        some = slice(*part)
        down_copies.append(axial_part(u, rows - 4, 0, 0, k, some, axial + 1))
        up_copies.append(axial_part(u, 0, 4, 0, k, some, axial - 1))
        soon_copies.append(axial_part(state_hbm, 0, 4, 0, k, some, axial - 1))

    def wait_axial(some, k, wait):
        for ways, flag in ((1, jnp.not_equal(has_up, has_down)), (2, both(has_up, has_down))):
            whole = ax_got.at[some, :, : 4 * ways, :]
            when(flag, lambda: wait(remote(whole, whole, 0, k, axial=axial)))

    slots = len(parts)
    got_left, got_right = got_sides.at[0], got_sides.at[1]
    right_copy = remote(sp_right, got_left, 1, slots, span=span + 1)
    left_copies = []
    for k, part in enumerate(span_parts):
        some = slice(*part)
        left_copies.append(
            remote(sp_left.at[some], got_right.at[some], 1, slots + 1 + k, span=span - 1)
        )

    def wait_span_sent():
        for ways, flag in (
            (1, jnp.not_equal(has_left, has_right)),
            (2, both(has_left, has_right)),
        ):
            whole = got_sides.at[:ways]
            when(flag, lambda: remote(whole, whole, 1, slots, span=span).wait_send())

    slots = slots + 1 + len(span_parts)

    def start_all(copies):
        for copy in copies:
            copy.start()

    held = both(under_hub, first, has_left)
    when(odd, lambda: start_all(soon_copies[:-1]))
    when(both(odd, no(held)), soon_copies[-1].start)
    if paired:
        when(far_hub, lambda: tell(next_ready, axial=axial - 2, pitch=pitch - 1))
    when(hub, lambda: tell(next_ready, axial=axial + 1))
    when(both(under_hub, first), lambda: tell(next_ready, axial=axial - 1))
    when(has_left, lambda: tell(side_ready, span=span - 1))
    for other in range(1, npitch):
        when(other > pitch, lambda: tell(side_ready, pitch=jnp.int32(other)))
    row = lax.broadcasted_iota(jnp.int32, (8, 128), 0)
    lane = lax.broadcasted_iota(jnp.int32, (8, 128), 1)
    group, place = lane // 4, lane % 4
    low_rows = row < 4

    late = both(even, no(both(hub_block, first)))

    @pl.when(late)
    def _():
        for copy in part_copies:
            copy.wait()
        when(has_up, lambda: start_all(up_copies))
        when(has_down, lambda: start_all(down_copies))

    groups = sp_left.shape[1]

    def pack_span(f, carry):
        for g in range(groups):
            right = left = jnp.zeros((8, 128), jnp.float32)
            for k in range(32):
                i, t = divmod(g * 32 + k, tiles)
                moved = pltpu.roll(u[f, i, t * 8 : t * 8 + 8, :], (4 * k + 4) % 128, 1)
                right = jnp.where(group == k, moved, right)
                left = jnp.where(group == (k + 1) % 32, moved, left)
            sp_right[f, g] = right
            sp_left[f, g] = left
        return carry

    for k, part in enumerate(span_parts):
        when(no(late), part_copies[k].wait)
        for f in range(*part):
            pack_span(f, 0)
        when(has_left, left_copies[k].start)
    when(both(even, has_up, no(late)), lambda: start_all(up_copies))
    coef_copy.start()
    lag_copy.start()

    ahead = both(under_hub, second, has_left)

    @pl.when(ahead)
    def _():
        pl.semaphore_wait(next_ready, 1)
        start_all(down_copies)

    def flux_tile(t, carry):
        at = pl.ds(pl.multiple_of(t * 8, 8), 8)
        parts = [None] * 4
        for i in range(cells):
            cell = [u[f, i, at, :] for f in range(fields)]
            inverse = 1.0 / cell[0]
            speed = cell[2] * inverse
            kinetic = 0.5 * (cell[1] * cell[1] + cell[2] * cell[2] + cell[3] * cell[3]) * inverse
            pressure = (HEAT_RATIO_GAS - 1.0) * (cell[4] - kinetic)
            values = [
                cell[2],
                cell[1] * speed,
                cell[2] * speed + pressure,
                cell[3] * speed,
                (cell[4] + pressure) * speed,
            ]
            for f in range(fields):
                flux[f, i, at, :] = values[f]
            if i == 0:
                parts = [list(values), list(values), list(cell), list(cell)]
            else:
                for f in range(fields):
                    parts[0][f] = r * parts[0][f] + values[f]
                    parts[1][f] = parts[1][f] + (r**i) * values[f]
                    parts[2][f] = q * parts[2][f] + cell[f]
                    parts[3][f] = parts[3][f] + (q**i) * cell[f]
        for s in range(4):
            for f in range(fields):
                sums[s, f, at, :] = parts[s][f]
        return carry

    lax.fori_loop(0, tiles, flux_tile, 0, unroll=True)

    sum_copies = [
        remote(sums, got_sums.at[step - 1], 1 + step, slots - 1 + step, pitch=lax.rem(pitch + step, npitch))
        for step in range(1, npitch)
    ]
    when(pitch == 0, lambda: start_all(sum_copies))

    def clear(ref):
        ref[...] = jnp.zeros_like(ref)

    when(no(has_up), lambda: clear(ax_got.at[:, :, :4, :]))
    when(no(has_down), lambda: clear(ax_got.at[:, :, 4:, :]))
    when(no(has_left), lambda: clear(got_left))
    when(no(has_right), lambda: clear(got_right))

    weight = -DAMPING / 256.0

    def damp_field(f, carry):
        for i in range(cells):
            x = u[f, i]
            result = (140.0 * weight) * x
            for o, c in ((1, -56.0), (2, 28.0), (3, -8.0), (4, 1.0)):
                pair = (pltpu.roll(x, o, 0) + pltpu.roll(x, rows - o, 0)) + (
                    pltpu.roll(x, o, 1) + pltpu.roll(x, 128 - o, 1)
                )
                result = result + (c * weight) * pair
            out_ref[f, i] = result
            ends = jnp.where(low_rows, x[:8, :], x[rows - 8 :, :])
            ax_own[f, i] = -pltpu.roll(ends, 4, 0)
        return carry

    behind = both(under_hub, second, no(has_left))

    @pl.when(both(jnp.logical_or(both(under_hub, no(ahead)), both(hub_block, first)), no(behind)))
    def _():
        pl.semaphore_wait(next_ready, 1)
        start_all(down_copies[:-1])
        when(held, soon_copies[-1].start)
        down_copies[-1].start()

    lag_copy.wait()
    harm_copy.start()

    damp_field(0, 0)
    damp_field(1, 0)

    @pl.when(behind)
    def _():
        pl.semaphore_wait(next_ready, 1)
        start_all(down_copies)

    sides = pitch + count(has_right)
    when(sides > 0, lambda: pl.semaphore_wait(side_ready, sides))
    when(pitch > 0, lambda: start_all(sum_copies))
    when(has_right, right_copy.start)

    for f in range(2, fields):
        damp_field(f, 0)

    harm_copy.wait()
    order = row.astype(jnp.float32) + 1.0
    phase = (2.0 * math.pi / PERIOD_SAMPLES) * order * lag_ref[0].astype(jnp.float32)
    active = row < harm_ref[...]
    waves[0] = jnp.where(active, jnp.cos(phase), 0.0)
    waves[1] = jnp.where(active, jnp.sin(phase), 0.0)
    near_first = pick(pitch, [r ** (cells * p) for p in range(npitch)])
    near_last = pick(pitch, [r ** (cells * (npitch - 1 - p)) for p in range(npitch)])
    jump_scale = -STEP_RATE * 0.75 * r_scale / (1.0 - r**total)
    jump_weights = [
        near_first * (jump_scale * (r**i + r ** (i + 1)))
        + near_last * (jump_scale * (r ** (cells - i) + r ** (cells - 1 - i)))
        for i in range(cells)
    ]
    flux_scale = -STEP_RATE * 0.75 * r_scale * (r - 1.0 / r)

    coef_copy.wait()

    def solve_field(f, carry):
        for t in range(tiles):
            at = pl.ds(t * 8, 8)
            jump = None
            for part in range(2):
                for k in range(harm_max):
                    term = waves[part, pl.ds(k, 1), :] * co[part, k, f, at, :]
                    jump = term if jump is None else jump + term
            x = [u[f, i, at, :] for i in range(cells)]
            y = [flux[f, i, at, :] for i in range(cells)]
            back_x, back_y = [None] * cells, [None] * cells
            carry_x, carry_y = q * x[cells - 1], y[cells - 1]
            for i in reversed(range(cells - 1)):
                back_x[i], back_y[i] = carry_x, carry_y
                if i > 0:
                    carry_x = q * (x[i] + carry_x)
                    carry_y = y[i] + r * carry_y
            front_x, front_y = None, None
            for i in range(cells):
                front_x = x[i] if front_x is None else x[i] + q * front_x
                value = out_ref[f, i, at, :] + jump_weights[i] * jump
                relaxed = front_x if back_x[i] is None else front_x + back_x[i]
                value = value + q_scale * relaxed
                slope = front_y
                if back_y[i] is not None:
                    slope = -back_y[i] if slope is None else slope - back_y[i]
                value = value + (flux_scale * r) * slope
                front_y = y[i] if front_y is None else y[i] + r * front_y
                out_ref[f, i, at, :] = value
        return carry

    lax.fori_loop(0, fields, solve_field, 0, unroll=True)

    for copy in sum_copies:
        copy.wait_recv()
    r_wrap = 1.0 / (1.0 - r**total)
    q_wrap = 1.0 / (1.0 - q**total)

    def carry_field(f, carry):
        for t in range(tiles):
            at = pl.ds(t * 8, 8)
            joined = []
            for s, (root, wrap) in enumerate(
                ((r, r_wrap), (r, r_wrap), (q, q_wrap), (q, q_wrap))
            ):
                value = (wrap * root ** (cells * (npitch - 1))) * sums[s, f, at, :]
                for step in range(1, npitch):
                    distance = step - 1 if s % 2 == 0 else npitch - 1 - step
                    factor = wrap * root ** (cells * distance)
                    value = value + factor * got_sums[step - 1, s, f, at, :]
                joined.append(value)
            for i in range(cells):
                out_ref[f, i, at, :] = (
                    out_ref[f, i, at, :]
                    + (flux_scale * r ** (i + 1)) * joined[0]
                    - (flux_scale * r ** (cells - i)) * joined[1]
                    + (q_scale * q ** (i + 1)) * joined[2]
                    + (q_scale * q ** (cells - i)) * joined[3]
                )
        return carry

    lax.fori_loop(0, fields, carry_field, 0, unroll=True)

    outer = jnp.logical_or(lane < 4, lane >= 124)
    from_left = [jnp.where(place + t < 4, EDGE[t] * weight, 0.0) for t in range(4)]
    from_right = [jnp.where(place >= t, EDGE[t] * weight, 0.0) for t in range(4)]
    even_group = group % 2 == 0

    def span_field(f, carry):
        for g in range(groups):
            before = got_left[f, g] - sp_right[f, g]
            after = got_right[f, g] - sp_left[f, g]
            starts, stops = from_left[0] * before, from_right[0] * after
            for t in range(1, 4):
                starts = starts + from_left[t] * pltpu.roll(before, 128 - t, 1)
                stops = stops + from_right[t] * pltpu.roll(after, t, 1)
            stops = pltpu.roll(stops, 120, 1)
            ends = (
                jnp.where(even_group, starts, stops),
                jnp.where(even_group, stops, starts),
            )
            for k in range(32):
                i, t = divmod(g * 32 + k, tiles)
                moved = pltpu.roll(ends[k % 2], (128 - 4 * k) % 128, 1)
                out_ref[f, i, t * 8 : t * 8 + 8, :] += jnp.where(outer, moved, 0.0)
        return carry

    def span_ends():
        when(has_left, right_copy.wait_recv)
        for k, part in enumerate(span_parts):
            when(has_right, left_copies[k].wait_recv)
            for f in range(*part):
                span_field(f, 0)

    corner = both(axial == 0, span == 0)
    when(no(corner), span_ends)

    near_low = [jnp.where(row + t < 4, EDGE[t] * weight, 0.0) for t in range(1, 4)]
    near_high = [jnp.where(row >= 4 + t, EDGE[t] * weight, 0.0) for t in range(1, 4)]

    def axial_field(f, carry):
        for i in range(cells):
            delta = ax_got[f, i] + ax_own[f, i]
            ends = (EDGE[0] * weight) * delta
            for t in range(1, 4):
                ends = ends + near_low[t - 1] * pltpu.roll(delta, 8 - t, 0)
                ends = ends + near_high[t - 1] * pltpu.roll(delta, t, 0)
            out_ref[f, i, :8, :] += jnp.where(low_rows, ends, 0.0)
            out_ref[f, i, rows - 8 :, :] += jnp.where(low_rows, 0.0, ends)
        return carry

    for k, part in enumerate(parts):
        wait_axial(slice(*part), k, lambda copy: copy.wait_recv())
        for f in range(*part):
            axial_field(f, 0)

    when(corner, span_ends)
    for copy in sum_copies:
        copy.wait_send()
    wait_axial(slice(0, fields), 0, lambda copy: copy.wait_send())
    wait_span_sent()


def shards(sizes, state, coeffs, lag_shift, harmonics):
    fields, cells, rows, lanes = state.shape
    npitch = sizes[0]
    groups = cells * (rows // 8) // 32
    vmem = lambda *shape: pltpu.VMEM(shape, jnp.float32)
    halo = (fields, cells, 8, lanes)
    packed = (fields, groups, 8, lanes)
    arrivals = len(split(fields, *AXIAL_CUTS)) + 1 + len(split(fields, *SPAN_CUTS)) + npitch - 1
    return pl.pallas_call(
        functools.partial(kernel, sizes),
        out_shape=pltpu.VMEM(state.shape, jnp.float32),
        in_specs=[
            pl.BlockSpec(memory_space=pltpu.HBM),
            pl.BlockSpec(memory_space=pltpu.HBM),
            pl.BlockSpec(memory_space=pltpu.HBM),
            pl.BlockSpec(memory_space=pltpu.HBM),
        ],
        out_specs=pl.BlockSpec(memory_space=pltpu.VMEM),
        scratch_shapes=[
            vmem(*state.shape),
            vmem(*coeffs.shape),
            vmem(*state.shape),
            vmem(4, fields, rows, lanes),
            vmem(npitch - 1, 4, fields, rows, lanes),
            vmem(*halo),
            vmem(*halo),
            vmem(*packed),
            vmem(*packed),
            vmem(2, *packed),
            vmem(2, 8, lanes),
            pltpu.SMEM((1,), jnp.int32),
            pltpu.VMEM((1, lanes), jnp.int32),
            pltpu.SemaphoreType.REGULAR,
            pltpu.SemaphoreType.REGULAR,
            pltpu.SemaphoreType.DMA((2,)),
            pltpu.SemaphoreType.DMA((2 + npitch - 1,)),
            pltpu.SemaphoreType.DMA((arrivals,)),
        ],
        compiler_params=pltpu.CompilerParams(collective_id=0, has_side_effects=True),
    )(lag_shift, harmonics.reshape(1, lanes), state, coeffs)


def solution(mesh):
    sizes = tuple(mesh.shape[name] for name in ("pitch", "axial", "span"))
    placed = (
        P(None, "pitch", "axial", "span"),
        P(None, None, None, "axial", "span"),
        P(),
        P("span"),
    )
    return jax.shard_map(
        functools.partial(shards, sizes),
        mesh=mesh,
        in_specs=placed,
        out_specs=P(None, "pitch", "axial", "span"),
        check_vma=False,
    )
```

```python
import functools
import math

import jax
import jax.numpy as jnp
from jax import lax
from jax.experimental import pallas as pl
from jax.experimental.pallas import tpu as pltpu
from jax.sharding import PartitionSpec as P

PERIOD_SAMPLES = 64
HEAT_RATIO_GAS = 1.4
STEP_RATE = 0.25
DAMPING = 0.5
EDGE = (1.0, -8.0, 28.0, -56.0)
MESH = pl.DeviceIdType.MESH
AXIAL_CUTS, SPAN_CUTS = (4,), (2,)


def line_root(main, side):
    root = (-main + math.sqrt(main * main - 4.0 * side * side)) / (2.0 * side)
    return root, 1.0 / (main + 2.0 * side * root)


def split(fields, *fifths):
    cuts = sorted({0, *(fields * n // 5 for n in fifths), fields})
    return tuple(zip(cuts[:-1], cuts[1:]))


def pick(position, values):
    chosen = jnp.float32(values[-1])
    for index in range(len(values) - 1):
        chosen = jnp.where(position == index, jnp.float32(values[index]), chosen)
    return chosen


def kernel(
    sizes,
    lag_hbm,
    harm_hbm,
    state_hbm,
    coef_hbm,
    out_ref,
    u,
    co,
    flux,
    sums,
    got_sums,
    ax_own,
    ax_got,
    sp_left,
    sp_right,
    got_sides,
    waves,
    lag_ref,
    harm_ref,
    side_ready,
    next_ready,
    local_sem,
    send_sem,
    recv_sem,
):
    npitch, naxial, nspan = sizes
    fields, cells, rows, _ = u.shape
    tiles = rows // 8
    parts, span_parts = split(fields, *AXIAL_CUTS), split(fields, *SPAN_CUTS)
    harm_max = co.shape[1]
    total = cells * npitch
    diffusion = float(total * total // 64)
    r, r_scale = line_root(1.0, 0.25)
    q, q_scale = line_root(1.0 + 2.0 * diffusion, -diffusion)
    pitch, axial, span = (lax.axis_index(name) for name in ("pitch", "axial", "span"))

    pair = 2 if cells % 2 == 0 else 1
    state_copies, part_copies = [], []
    for k, part in enumerate(span_parts):
        some = slice(*part)
        part_copies.append(pltpu.make_async_copy(state_hbm.at[some], u.at[some], local_sem.at[k]))
        for f in range(*part):
            for i in range(0, cells, pair):
                some = (f, slice(i, i + pair))
                state_copies.append(
                    pltpu.make_async_copy(state_hbm.at[some], u.at[some], local_sem.at[k])
                )
    coef_copy = pltpu.make_async_copy(coef_hbm, co, local_sem.at[0])
    lag_copy = pltpu.make_async_copy(lag_hbm, lag_ref, local_sem.at[1])
    harm_copy = pltpu.make_async_copy(harm_hbm, harm_ref, local_sem.at[1])

    def when(flag, action):
        @pl.when(flag)
        def _():
            action()

    def both(*flags):
        return functools.reduce(jnp.logical_and, flags)

    def no(flag):
        return jnp.logical_not(flag)

    paired = npitch % 2 == 0 and naxial % 2 == 0
    has_up, has_down = axial > 0, axial < naxial - 1
    has_left, has_right = span > 0, span < nspan - 1
    odd = lax.rem(axial, 2) == 1
    even = no(odd)
    hub_block = both(even, axial + 2 < naxial)
    last_even = both(even, axial + 2 >= naxial)
    second = lax.rem(pitch, 2) == 1 if paired else pitch >= 0
    first = no(second)
    hub = both(hub_block, second)
    far_hub = both(odd, second, axial > 2)
    under_hub = both(odd, has_down)

    barrier = pltpu.get_barrier_semaphore()

    def tell(semaphore, **where):
        pl.semaphore_signal(semaphore, inc=1, device_id=where, device_id_type=MESH)

    def count(*flags):
        return sum(jnp.where(flag, 1, 0) for flag in flags)

    told_axial, told_pitch = jnp.where(odd, axial - 1, axial - 2), pitch
    if paired:
        told_axial = jnp.where(both(first, even), axial + 1, told_axial)
        told_axial = jnp.where(both(first, under_hub), axial + 2, told_axial)
        told_pitch = jnp.where(both(first, jnp.logical_or(even, has_down)), pitch + 1, pitch)
    when(has_up, lambda: tell(barrier, axial=told_axial, pitch=told_pitch))
    when(has_down, lambda: tell(barrier, axial=axial + 1))
    for copy in state_copies:
        copy.start()
    when(has_right, lambda: tell(barrier, span=span + 1))
    for other in range(npitch - 1):
        when(other < pitch, lambda: tell(barrier, pitch=jnp.int32(other)))

    heard = count(has_left, has_up, both(last_even, has_down))
    heard = heard + 2 * count(hub) + (npitch - 1 - pitch)
    if paired:
        heard = heard + 2 * count(far_hub)
    pl.semaphore_wait(barrier, heard)

    def remote(src, dst, sent, got, **where):
        return pltpu.make_async_remote_copy(
            src_ref=src,
            dst_ref=dst,
            send_sem=send_sem.at[sent],
            recv_sem=recv_sem.at[got],
            device_id=where,
            device_id_type=MESH,
        )

    def axial_part(src, from_row, to_row, sent, got, some, target):
        return remote(
            src.at[some, :, from_row : from_row + 4, :],
            ax_got.at[some, :, to_row : to_row + 4, :],
            sent,
            got,
            axial=target,
        )

    down_copies, up_copies, soon_copies = [], [], []
    for k, part in enumerate(parts):
        some = slice(*part)
        down_copies.append(axial_part(u, rows - 4, 0, 0, k, some, axial + 1))
        up_copies.append(axial_part(u, 0, 4, 0, k, some, axial - 1))
        soon_copies.append(axial_part(state_hbm, 0, 4, 0, k, some, axial - 1))

    def wait_axial(some, k, wait):
        for ways, flag in ((1, jnp.not_equal(has_up, has_down)), (2, both(has_up, has_down))):
            whole = ax_got.at[some, :, : 4 * ways, :]
            when(flag, lambda: wait(remote(whole, whole, 0, k, axial=axial)))

    slots = len(parts)
    got_left, got_right = got_sides.at[0], got_sides.at[1]
    right_copy = remote(sp_right, got_left, 1, slots, span=span + 1)
    left_copies = []
    for k, part in enumerate(span_parts):
        some = slice(*part)
        left_copies.append(
            remote(sp_left.at[some], got_right.at[some], 1, slots + 1 + k, span=span - 1)
        )

    def wait_span_sent():
        for ways, flag in (
            (1, jnp.not_equal(has_left, has_right)),
            (2, both(has_left, has_right)),
        ):
            whole = got_sides.at[:ways]
            when(flag, lambda: remote(whole, whole, 1, slots, span=span).wait_send())

    slots = slots + 1 + len(span_parts)

    def start_all(copies):
        for copy in copies:
            copy.start()

    if paired:
        when(far_hub, lambda: tell(next_ready, axial=axial - 2, pitch=pitch - 1))
    when(hub, lambda: tell(next_ready, axial=axial + 1))
    held = both(under_hub, first, has_left)
    when(odd, lambda: start_all(soon_copies[:-1]))
    when(both(odd, no(held)), soon_copies[-1].start)
    when(both(under_hub, first), lambda: tell(next_ready, axial=axial - 1))
    when(has_left, lambda: tell(side_ready, span=span - 1))
    for other in range(1, npitch):
        when(other > pitch, lambda: tell(side_ready, pitch=jnp.int32(other)))
    row = lax.broadcasted_iota(jnp.int32, (8, 128), 0)
    lane = lax.broadcasted_iota(jnp.int32, (8, 128), 1)
    group, place = lane // 4, lane % 4
    low_rows = row < 4

    late = both(even, no(both(hub_block, first)))

    @pl.when(late)
    def _():
        for copy in part_copies:
            copy.wait()
        when(has_up, lambda: start_all(up_copies))
        when(has_down, lambda: start_all(down_copies))

    groups = sp_left.shape[1]

    def pack_span(f, carry):
        for g in range(groups):
            right = left = jnp.zeros((8, 128), jnp.float32)
            for k in range(32):
                i, t = divmod(g * 32 + k, tiles)
                moved = pltpu.roll(u[f, i, t * 8 : t * 8 + 8, :], (4 * k + 4) % 128, 1)
                right = jnp.where(group == k, moved, right)
                left = jnp.where(group == (k + 1) % 32, moved, left)
            sp_right[f, g] = right
            sp_left[f, g] = left
        return carry

    for k, part in enumerate(span_parts):
        when(no(late), part_copies[k].wait)
        for f in range(*part):
            pack_span(f, 0)
        when(has_left, left_copies[k].start)
    when(both(even, has_up, no(late)), lambda: start_all(up_copies))
    coef_copy.start()
    lag_copy.start()

    ahead = both(under_hub, second, has_left)

    @pl.when(ahead)
    def _():
        pl.semaphore_wait(next_ready, 1)
        start_all(down_copies)

    def flux_tile(t, carry):
        at = pl.ds(pl.multiple_of(t * 8, 8), 8)
        parts = [None] * 4
        for i in range(cells):
            cell = [u[f, i, at, :] for f in range(fields)]
            inverse = 1.0 / cell[0]
            speed = cell[2] * inverse
            kinetic = 0.5 * (cell[1] * cell[1] + cell[2] * cell[2] + cell[3] * cell[3]) * inverse
            pressure = (HEAT_RATIO_GAS - 1.0) * (cell[4] - kinetic)
            values = [
                cell[2],
                cell[1] * speed,
                cell[2] * speed + pressure,
                cell[3] * speed,
                (cell[4] + pressure) * speed,
            ]
            for f in range(fields):
                flux[f, i, at, :] = values[f]
            if i == 0:
                parts = [list(values), list(values), list(cell), list(cell)]
            else:
                for f in range(fields):
                    parts[0][f] = r * parts[0][f] + values[f]
                    parts[1][f] = parts[1][f] + (r**i) * values[f]
                    parts[2][f] = q * parts[2][f] + cell[f]
                    parts[3][f] = parts[3][f] + (q**i) * cell[f]
        for s in range(4):
            for f in range(fields):
                sums[s, f, at, :] = parts[s][f]
        return carry

    lax.fori_loop(0, tiles, flux_tile, 0, unroll=True)

    sum_copies = [
        remote(sums, got_sums.at[step - 1], 1 + step, slots - 1 + step, pitch=lax.rem(pitch + step, npitch))
        for step in range(1, npitch)
    ]
    when(pitch == 0, lambda: start_all(sum_copies))

    def clear(ref):
        ref[...] = jnp.zeros_like(ref)

    when(no(has_up), lambda: clear(ax_got.at[:, :, :4, :]))
    when(no(has_down), lambda: clear(ax_got.at[:, :, 4:, :]))
    when(no(has_left), lambda: clear(got_left))
    when(no(has_right), lambda: clear(got_right))

    weight = -DAMPING / 256.0

    def damp_field(f, carry):
        for i in range(cells):
            x = u[f, i]
            result = (140.0 * weight) * x
            for o, c in ((1, -56.0), (2, 28.0), (3, -8.0), (4, 1.0)):
                pair = (pltpu.roll(x, o, 0) + pltpu.roll(x, rows - o, 0)) + (
                    pltpu.roll(x, o, 1) + pltpu.roll(x, 128 - o, 1)
                )
                result = result + (c * weight) * pair
            out_ref[f, i] = result
            ends = jnp.where(low_rows, x[:8, :], x[rows - 8 :, :])
            ax_own[f, i] = -pltpu.roll(ends, 4, 0)
        return carry

    behind = both(under_hub, second, no(has_left))

    @pl.when(both(jnp.logical_or(both(under_hub, no(ahead)), both(hub_block, first)), no(behind)))
    def _():
        pl.semaphore_wait(next_ready, 1)
        start_all(down_copies[:-1])
        when(held, soon_copies[-1].start)
        down_copies[-1].start()

    lag_copy.wait()
    harm_copy.start()

    damp_field(0, 0)
    damp_field(1, 0)

    @pl.when(behind)
    def _():
        pl.semaphore_wait(next_ready, 1)
        start_all(down_copies)

    sides = pitch + count(has_right)
    when(sides > 0, lambda: pl.semaphore_wait(side_ready, sides))
    when(pitch > 0, lambda: start_all(sum_copies))
    when(has_right, right_copy.start)

    for f in range(2, fields):
        damp_field(f, 0)

    harm_copy.wait()
    order = row.astype(jnp.float32) + 1.0
    phase = (2.0 * math.pi / PERIOD_SAMPLES) * order * lag_ref[0].astype(jnp.float32)
    active = row < harm_ref[...]
    waves[0] = jnp.where(active, jnp.cos(phase), 0.0)
    waves[1] = jnp.where(active, jnp.sin(phase), 0.0)
    near_first = pick(pitch, [r ** (cells * p) for p in range(npitch)])
    near_last = pick(pitch, [r ** (cells * (npitch - 1 - p)) for p in range(npitch)])
    jump_scale = -STEP_RATE * 0.75 * r_scale / (1.0 - r**total)
    jump_weights = [
        near_first * (jump_scale * (r**i + r ** (i + 1)))
        + near_last * (jump_scale * (r ** (cells - i) + r ** (cells - 1 - i)))
        for i in range(cells)
    ]
    flux_scale = -STEP_RATE * 0.75 * r_scale * (r - 1.0 / r)

    coef_copy.wait()

    def solve_field(f, carry):
        for t in range(tiles):
            at = pl.ds(t * 8, 8)
            jump = None
            for part in range(2):
                for k in range(harm_max):
                    term = waves[part, pl.ds(k, 1), :] * co[part, k, f, at, :]
                    jump = term if jump is None else jump + term
            x = [u[f, i, at, :] for i in range(cells)]
            y = [flux[f, i, at, :] for i in range(cells)]
            back_x, back_y = [None] * cells, [None] * cells
            carry_x, carry_y = q * x[cells - 1], y[cells - 1]
            for i in reversed(range(cells - 1)):
                back_x[i], back_y[i] = carry_x, carry_y
                if i > 0:
                    carry_x = q * (x[i] + carry_x)
                    carry_y = y[i] + r * carry_y
            front_x, front_y = None, None
            for i in range(cells):
                front_x = x[i] if front_x is None else x[i] + q * front_x
                value = out_ref[f, i, at, :] + jump_weights[i] * jump
                relaxed = front_x if back_x[i] is None else front_x + back_x[i]
                value = value + q_scale * relaxed
                slope = front_y
                if back_y[i] is not None:
                    slope = -back_y[i] if slope is None else slope - back_y[i]
                value = value + (flux_scale * r) * slope
                front_y = y[i] if front_y is None else y[i] + r * front_y
                out_ref[f, i, at, :] = value
        return carry

    lax.fori_loop(0, fields, solve_field, 0, unroll=True)

    for copy in sum_copies:
        copy.wait_recv()
    r_wrap = 1.0 / (1.0 - r**total)
    q_wrap = 1.0 / (1.0 - q**total)

    def carry_field(f, carry):
        for t in range(tiles):
            at = pl.ds(t * 8, 8)
            joined = []
            for s, (root, wrap) in enumerate(
                ((r, r_wrap), (r, r_wrap), (q, q_wrap), (q, q_wrap))
            ):
                value = (wrap * root ** (cells * (npitch - 1))) * sums[s, f, at, :]
                for step in range(1, npitch):
                    distance = step - 1 if s % 2 == 0 else npitch - 1 - step
                    factor = wrap * root ** (cells * distance)
                    value = value + factor * got_sums[step - 1, s, f, at, :]
                joined.append(value)
            for i in range(cells):
                out_ref[f, i, at, :] = (
                    out_ref[f, i, at, :]
                    + (flux_scale * r ** (i + 1)) * joined[0]
                    - (flux_scale * r ** (cells - i)) * joined[1]
                    + (q_scale * q ** (i + 1)) * joined[2]
                    + (q_scale * q ** (cells - i)) * joined[3]
                )
        return carry

    lax.fori_loop(0, fields, carry_field, 0, unroll=True)

    outer = jnp.logical_or(lane < 4, lane >= 124)
    from_left = [jnp.where(place + t < 4, EDGE[t] * weight, 0.0) for t in range(4)]
    from_right = [jnp.where(place >= t, EDGE[t] * weight, 0.0) for t in range(4)]
    even_group = group % 2 == 0

    def span_field(f, carry):
        for g in range(groups):
            before = got_left[f, g] - sp_right[f, g]
            after = got_right[f, g] - sp_left[f, g]
            starts, stops = from_left[0] * before, from_right[0] * after
            for t in range(1, 4):
                starts = starts + from_left[t] * pltpu.roll(before, 128 - t, 1)
                stops = stops + from_right[t] * pltpu.roll(after, t, 1)
            stops = pltpu.roll(stops, 120, 1)
            ends = (
                jnp.where(even_group, starts, stops),
                jnp.where(even_group, stops, starts),
            )
            for k in range(32):
                i, t = divmod(g * 32 + k, tiles)
                moved = pltpu.roll(ends[k % 2], (128 - 4 * k) % 128, 1)
                out_ref[f, i, t * 8 : t * 8 + 8, :] += jnp.where(outer, moved, 0.0)
        return carry

    def span_ends():
        when(has_left, right_copy.wait_recv)
        for k, part in enumerate(span_parts):
            when(has_right, left_copies[k].wait_recv)
            for f in range(*part):
                span_field(f, 0)

    corner = both(axial == 0, span == 0)
    when(no(corner), span_ends)

    near_low = [jnp.where(row + t < 4, EDGE[t] * weight, 0.0) for t in range(1, 4)]
    near_high = [jnp.where(row >= 4 + t, EDGE[t] * weight, 0.0) for t in range(1, 4)]

    def axial_field(f, carry):
        for i in range(cells):
            delta = ax_got[f, i] + ax_own[f, i]
            ends = (EDGE[0] * weight) * delta
            for t in range(1, 4):
                ends = ends + near_low[t - 1] * pltpu.roll(delta, 8 - t, 0)
                ends = ends + near_high[t - 1] * pltpu.roll(delta, t, 0)
            out_ref[f, i, :8, :] += jnp.where(low_rows, ends, 0.0)
            out_ref[f, i, rows - 8 :, :] += jnp.where(low_rows, 0.0, ends)
        return carry

    for k, part in enumerate(parts):
        wait_axial(slice(*part), k, lambda copy: copy.wait_recv())
        for f in range(*part):
            axial_field(f, 0)

    when(corner, span_ends)
    for copy in sum_copies:
        copy.wait_send()
    wait_axial(slice(0, fields), 0, lambda copy: copy.wait_send())
    wait_span_sent()


def shards(sizes, state, coeffs, lag_shift, harmonics):
    fields, cells, rows, lanes = state.shape
    npitch = sizes[0]
    groups = cells * (rows // 8) // 32
    vmem = lambda *shape: pltpu.VMEM(shape, jnp.float32)
    halo = (fields, cells, 8, lanes)
    packed = (fields, groups, 8, lanes)
    arrivals = len(split(fields, *AXIAL_CUTS)) + 1 + len(split(fields, *SPAN_CUTS)) + npitch - 1
    return pl.pallas_call(
        functools.partial(kernel, sizes),
        out_shape=pltpu.VMEM(state.shape, jnp.float32),
        in_specs=[
            pl.BlockSpec(memory_space=pltpu.HBM),
            pl.BlockSpec(memory_space=pltpu.HBM),
            pl.BlockSpec(memory_space=pltpu.HBM),
            pl.BlockSpec(memory_space=pltpu.HBM),
        ],
        out_specs=pl.BlockSpec(memory_space=pltpu.VMEM),
        scratch_shapes=[
            vmem(*state.shape),
            vmem(*coeffs.shape),
            vmem(*state.shape),
            vmem(4, fields, rows, lanes),
            vmem(npitch - 1, 4, fields, rows, lanes),
            vmem(*halo),
            vmem(*halo),
            vmem(*packed),
            vmem(*packed),
            vmem(2, *packed),
            vmem(2, 8, lanes),
            pltpu.SMEM((1,), jnp.int32),
            pltpu.VMEM((1, lanes), jnp.int32),
            pltpu.SemaphoreType.REGULAR,
            pltpu.SemaphoreType.REGULAR,
            pltpu.SemaphoreType.DMA((2,)),
            pltpu.SemaphoreType.DMA((2 + npitch - 1,)),
            pltpu.SemaphoreType.DMA((arrivals,)),
        ],
        compiler_params=pltpu.CompilerParams(collective_id=0, has_side_effects=True),
    )(lag_shift, harmonics.reshape(1, lanes), state, coeffs)


def solution(mesh):
    sizes = tuple(mesh.shape[name] for name in ("pitch", "axial", "span"))
    placed = (
        P(None, "pitch", "axial", "span"),
        P(None, None, None, "axial", "span"),
        P(),
        P("span"),
    )
    return jax.shard_map(
        functools.partial(shards, sizes),
        mesh=mesh,
        in_specs=placed,
        out_specs=P(None, "pitch", "axial", "span"),
        check_vma=False,
    )
```
